128 devices in a mesh: seq: 16 (over z, y_lo, core), grp: 8 (over y_hi, x).
Axes of the slice: x: 4, y: 4 (y_hi: 2, y_lo: 2; y = y_hi * 2 + y_lo), z: 4, core: 2. Of those that a mesh axis runs over, the one named last changes fastest.
Arguments:
- layer_input: bfloat16 [8, 8192, 4096], P('grp', 'seq'), may hold values from -6 to 6
- queries: bfloat16 [8, 8192, 2048], P('grp', 'seq'), may hold values from -6 to 6
- key_vectors: bfloat16 [8, 8192, 2048], P('grp', 'seq'), may hold values from -6 to 6
- value_vectors: bfloat16 [8, 8192, 2048], P('grp', 'seq'), may hold values from -6 to 6
- grad_output: bfloat16 [8, 8192, 2048], P('grp', 'seq'), may hold values from -0.015625 to 0.015625
Outputs:
- grad_queries: bfloat16 [8, 8192, 2048], P('grp', 'seq')
- grad_keys: bfloat16 [8, 8192, 2048], P('grp', 'seq')
- grad_values: bfloat16 [8, 8192, 2048], P('grp', 'seq')
- grad_weight: float32 [4096, 2048], P('seq', 'grp')
The draws below stay inside these ranges and needn't reach their ends.
All inputs are finite; a program needn't handle non-finite values.
Results may differ from the reference program's by a relative error of at most 0.0049.
Values sent between devices are 32-bit elements; how exact they have to be, the bound alone decides.
A program may use at most 192 MiB of HBM per device.

```python
import jax
import jax.numpy as jnp
from jax import lax

D = 4096
H = 16
HDIM = 128
BLK = 512
TOK_DEV = 512
HD = 2048
LENGTH = 8192
SEQS = 8
TOKENS = 65536
N_SEQ = 16


def with_spikes(drawn, stream_key, source, target, parts, factor):
    owner, partner = [(jnp.arange(drawn.shape[position]) // (drawn.shape[position] // parts)).reshape([-1 if axis == position else 1 for axis in range(drawn.ndim)]) for position in (source, target)]
    chosen = jax.random.permutation(stream_key, parts)[partner]
    strong = (owner == chosen) | (owner == (partner + parts // 2) % parts)
    return jnp.where(strong, factor * drawn, drawn)


def shard_levels(own_key, dims, cuts, low, top_value):
    loudness = 1.0
    for dim, shards_of in cuts:
        heights = jax.random.uniform(jax.random.fold_in(jax.random.fold_in(own_key, 6), dim), (shards_of,), jnp.float32, low / len(cuts), top_value / len(cuts))
        loudness = loudness * jnp.repeat(jnp.exp(heights), dims[dim] // shards_of).reshape((-1,) + (1,) * (len(dims) - 1 - dim))
    return loudness


def bell_draw(own_key, shape, width, limit, cuts=(), kind=jnp.bfloat16):
    level = shard_levels(own_key, shape, cuts, -0.22, 0.18) if cuts else 1.0
    result = jax.random.normal(own_key, shape, jnp.float32) * width * level
    return jnp.minimum(jnp.maximum(result, -limit), limit).astype(kind)


def heavy_noise(key, extent, spread, limit, cuts, heavy, kind=jnp.bfloat16):
    drawn = spread * jax.random.normal(key, extent, jnp.float32)
    if cuts:
        drawn = drawn * shard_levels(key, extent, cuts, -0.22, 0.18)
    return jnp.clip(with_spikes(drawn, jax.random.fold_in(key, 3), *heavy), -limit, limit).astype(kind)


def setup_inputs(seed: int = 0) -> dict:
    key_of = jax.random.split(jax.random.key(seed), 6)
    return {
        "layer_input": heavy_noise(key_of[0], (SEQS, LENGTH, D), 1.0, 6.0, ((0, 8), (1, 16)), (1, 2, 16, 2.0)),
        "queries": bell_draw(key_of[1], (SEQS, LENGTH, HD), 1.0, 6.0, ((0, 8), (1, 16))),
        "key_vectors": bell_draw(key_of[2], (SEQS, LENGTH, HD), 1.0, 6.0, ((0, 8), (1, 16))),
        "value_vectors": bell_draw(key_of[3], (SEQS, LENGTH, HD), 1.0, 6.0, ((0, 8), (1, 16))),
        "grad_output": bell_draw(key_of[4], (SEQS, LENGTH, HD), ((HDIM * LENGTH) ** -0.5), 0.015625, ((0, 8), (1, 16))),
    }


def rounded(array):
    return lax.optimization_barrier(array.astype(jnp.bfloat16)).astype(jnp.float32)


def sequence_grads(item):
    query_seq, key_seq, value_seq, grad_seq = item
    block_len = min(TOK_DEV, BLK)
    block_count = LENGTH // block_len

    def split(array):
        return array.astype(jnp.float32).reshape(block_count, block_len, H, HDIM)

    q_blocks = split(query_seq)
    k_blocks = split(key_seq)
    v_blocks = split(value_seq)
    g_blocks = split(grad_seq)
    kv_sum = jnp.einsum("bthe,bthf->bhef", k_blocks, v_blocks)
    qg_sum = jnp.einsum("bthe,bthf->bhef", q_blocks, g_blocks)
    before = jnp.cumsum(kv_sum, axis=0) - kv_sum
    after = jnp.sum(qg_sum, axis=0) - jnp.cumsum(qg_sum, axis=0)
    before_r = rounded(before)
    after_r = rounded(after)
    causal = jnp.tril(jnp.ones((block_len, block_len), dtype=bool))
    within = rounded(jnp.where(causal, jnp.einsum("bthe,bshe->bhts", q_blocks, k_blocks), 0.0))
    back = rounded(jnp.where(causal, jnp.einsum("bthf,bshf->bhts", g_blocks, v_blocks), 0.0))
    grad_q = jnp.einsum("bhts,bshe->bthe", back, k_blocks) + jnp.einsum("bthf,bhef->bthe", g_blocks, before_r)
    grad_k = jnp.einsum("bhts,bthe->bshe", back, q_blocks) + jnp.einsum("bshf,bhef->bshe", v_blocks, after_r)
    grad_v = jnp.einsum("bhts,bthf->bshf", within, g_blocks) + jnp.einsum("bshe,bhef->bshf", k_blocks, after_r)
    return (grad_q.astype(jnp.bfloat16).reshape(LENGTH, HD),
            grad_k.astype(jnp.bfloat16).reshape(LENGTH, HD),
            grad_v.astype(jnp.bfloat16).reshape(LENGTH, HD))


def reference(layer_input, queries, key_vectors, value_vectors, grad_output):
    grad_queries, grad_keys, grad_values = lax.map(sequence_grads, (queries, key_vectors, value_vectors, grad_output))
    run_count = SEQS * N_SEQ
    input_runs = layer_input.reshape(run_count, TOK_DEV, D)
    value_runs = grad_values.reshape(run_count, TOK_DEV, HD)

    def accumulate(total, pair):
        input_run, value_run = pair
        partial_value = jnp.dot(input_run.astype(jnp.float32).T, value_run.astype(jnp.float32), precision=lax.Precision.HIGHEST)
        return total + partial_value, None

    total, unused = lax.scan(accumulate, jnp.zeros((D, HD), jnp.float32), (input_runs, value_runs))
    grad_weight = total * (float(TOKENS) ** -0.5)
    return grad_queries, grad_keys, grad_values, grad_weight
```

```python
import jax
import jax.numpy as jnp
from jax import lax
from jax.experimental import pallas as pl
from jax.experimental.pallas import tpu as pltpu
from jax.sharding import PartitionSpec as P

MESH = pl.DeviceIdType.MESH
H = 16
HDIM = 128
BLK = 512
HD = 2048
F32 = jnp.float32
BF16 = jnp.bfloat16

ROWS = {
    (0, 0): (48, 40), (0, 1): (40, 48), (0, 2): (40, 40),
    (1, 0): (40, 48), (1, 1): (48, 40), (1, 2): (40, 40),
}
ORDER = (("x", "y", "z"), ("y", "z", "x"), ("z", "x", "y"))
UNITS = [(h, c, f) for h in range(2) for c in range(3) for f in range(2)]


def row_start(h, c, f):
    start = sum(sum(ROWS[(h, prior)]) for prior in range(c))
    return start + (ROWS[(h, c)][0] if f else 0)


def place():
    seq, grp = lax.axis_index("seq"), lax.axis_index("grp")
    core = lax.rem(seq, 2)
    y_lo = lax.rem(lax.div(seq, 2), 2)
    return {
        "x": lax.rem(grp, 4),
        "y": lax.div(grp, 4) * 2 + y_lo,
        "z": lax.div(seq, 4),
        "core": core,
    }


def device(at):
    return (
        at["z"] * 4 + lax.rem(at["y"], 2) * 2 + at["core"],
        lax.div(at["y"], 2) * 4 + at["x"],
    )


def shifted(at, axis, delta):
    moved = dict(at)
    moved[axis] = lax.rem(at[axis] + delta + 4, 4)
    return device(moved)


def partner_of(at):
    moved = dict(at)
    moved["core"] = 1 - at["core"]
    return device(moved)


def greet(devices):
    barrier = pltpu.get_barrier_semaphore()
    for other in devices:
        pl.semaphore_signal(barrier, inc=1, device_id=other, device_id_type=MESH)
    pl.semaphore_wait(barrier, len(devices))


def weight_kernel(xt_ref, dv_ref, out_ref, *scratch):
    parts = {unit: scratch[4 * i] for i, unit in enumerate(UNITS)}
    landing = {unit: scratch[4 * i + 1 : 4 * i + 4] for i, unit in enumerate(UNITS)}
    send_sem, recv_sem = scratch[4 * len(UNITS) :]
    at = place()
    greet([shifted(at, axis, delta) for axis in "xyz" for delta in (1, -1)])

    def view(unit, stage):
        ref = parts[unit]
        for earlier in range(stage):
            ref = ref.at[at[ORDER[unit[1]][earlier]]]
        return ref

    def hop(unit, stage, kind):
        index = UNITS.index(unit)
        axis = ORDER[unit[1]][stage]
        sign = 1 if unit[2] else -1
        mine = at[axis]
        chunk, toward = (
            (lax.rem(mine + 2, 4), sign),
            (lax.rem(mine - sign + 4, 4), -sign),
            (lax.rem(mine + sign + 4, 4), sign),
        )[kind]
        return pltpu.make_async_remote_copy(
            src_ref=view(unit, stage).at[chunk],
            dst_ref=landing[unit][stage].at[kind],
            send_sem=send_sem.at[index, stage, kind],
            recv_sem=recv_sem.at[index, stage, kind],
            device_id=shifted(at, axis, toward),
            device_id_type=MESH,
        )

    def compute(h):
        def block(b, carry):
            rows = pl.multiple_of(b * 256, 256)
            z, y_lo = lax.div(b, 2), lax.rem(b, 2)
            lhs = xt_ref[pl.ds(rows, 256), :]
            for pair in range(4):
                acc = jnp.dot(
                    lhs,
                    dv_ref[h, :, pair * 256 : pair * 256 + 256],
                    preferred_element_type=F32,
                )
                for side in range(2):
                    tile = 2 * pair + side
                    dest = {"x": tile % 4, "y": (tile // 4) * 2 + y_lo, "z": z}
                    for c in range(3):
                        for f in range(2):
                            start = row_start(h, c, f)
                            i, j, k = (dest[axis] for axis in ORDER[c])
                            parts[(h, c, f)][i, j, k] = acc[
                                start : start + ROWS[(h, c)][f],
                                side * 128 : side * 128 + 128,
                            ]
            return carry

        lax.fori_loop(0, 8, block, 0)

    def units_of(h):
        return [unit for unit in UNITS if unit[0] == h]

    def issue(h, stage):
        for kind in range(2):
            for unit in units_of(h):
                hop(unit, stage, kind).start()

    def combine(h, stage):
        for unit in units_of(h):
            axis = ORDER[unit[1]][stage]
            sign = 1 if unit[2] else -1
            hop(unit, stage, 0).wait_recv()
            target = view(unit, stage).at[lax.rem(at[axis] + sign + 4, 4)]
            arrived = landing[unit][stage].at[0]
            if stage == 0:
                def add(i, carry, target=target, arrived=arrived):
                    target[i] = target[i] + arrived[i]
                    return carry

                lax.fori_loop(0, 4, add, 0)
            else:
                target[...] = target[...] + arrived[...]
            hop(unit, stage, 2).start()

    def final(h, stage, then):
        for unit in units_of(h):
            axis = ORDER[unit[1]][stage]
            hop(unit, stage, 1).wait_recv()
            hop(unit, stage, 2).wait_recv()
            target = view(unit, stage).at[at[axis]]
            direct = landing[unit][stage].at[1]
            summed = landing[unit][stage].at[2]
            if stage == 0:
                def add(i, carry, target=target, direct=direct, summed=summed):
                    target[i] = target[i] + direct[i] + summed[i]
                    return carry

                lax.fori_loop(0, 4, add, 0)
            elif stage == 1:
                target[...] = target[...] + direct[...] + summed[...]
            else:
                start = row_start(*unit)
                total = target[...] + direct[...] + summed[...]
                out_ref[start : start + ROWS[unit[:2]][unit[2]], h * 128 : h * 128 + 128] = (
                    total * SCALE
                )
            if then:
                hop(unit, stage + 1, 0).start()
                hop(unit, stage + 1, 1).start()

    compute(0)
    issue(0, 0)
    compute(1)
    combine(0, 0)
    issue(1, 0)
    final(0, 0, True)
    combine(1, 0)
    combine(0, 1)
    final(0, 1, True)
    final(1, 0, True)
    combine(0, 2)
    final(0, 2, False)
    combine(1, 1)
    final(1, 1, True)
    combine(1, 2)
    final(1, 2, False)
    for unit in UNITS:
        for stage in range(3):
            for kind in range(3):
                hop(unit, stage, kind).wait_send()


SCALE = 65536.0 ** -0.5


def weight(xt, dvh):
    scratch = []
    for h, c, f in UNITS:
        r = ROWS[(h, c)][f]
        scratch.append(pltpu.VMEM((4, 4, 4, r, 128), F32))
        scratch.append(pltpu.VMEM((3, 4, 4, r, 128), F32))
        scratch.append(pltpu.VMEM((3, 4, r, 128), F32))
        scratch.append(pltpu.VMEM((3, r, 128), F32))
    scratch.append(pltpu.SemaphoreType.DMA((len(UNITS), 3, 3)))
    scratch.append(pltpu.SemaphoreType.DMA((len(UNITS), 3, 3)))
    return pl.pallas_call(
        weight_kernel,
        out_shape=jax.ShapeDtypeStruct((256, 256), F32),
        in_specs=[pl.BlockSpec(memory_space=pltpu.VMEM)] * 2,
        out_specs=pl.BlockSpec(memory_space=pltpu.VMEM),
        scratch_shapes=scratch,
        compiler_params=pltpu.CompilerParams(
            collective_id=1, has_side_effects=True, vmem_limit_bytes=60 << 20
        ),
        name="weight_rs",
    )(xt, dvh)


def pair_kernel(x_ref, dv_ref, xt_ref, dvh_ref, xs, xr, ds, dr, send_sem, recv_sem):
    at = place()
    core = at["core"]
    other = partner_of(at)
    greet([other])

    def copy_x(b):
        return pltpu.make_async_remote_copy(
            src_ref=xs.at[b], dst_ref=xr.at[b], send_sem=send_sem.at[b],
            recv_sem=recv_sem.at[b], device_id=other, device_id_type=MESH)

    def copy_d(h):
        return pltpu.make_async_remote_copy(
            src_ref=ds.at[h], dst_ref=dr.at[h], send_sem=send_sem.at[8 + h],
            recv_sem=recv_sem.at[8 + h], device_id=other, device_id_type=MESH)

    for h in range(2):
        for j in range(8):
            piece = dv_ref[:, (2 * j + h) * 128 : (2 * j + h) * 128 + 128]
            ds[h, :, j * 128 : j * 128 + 128] = piece.astype(F32)
            dvh_ref[h, 0:512, j * 128 : j * 128 + 128] = piece
        copy_d(h).start()

    def send_x(b, carry):
        cols = pl.multiple_of(b * 512 + (1 - core) * 256, 256)
        xs[b] = x_ref[:, pl.ds(cols, 256)].astype(F32)
        copy_x(b).start()
        return carry

    lax.fori_loop(0, 8, send_x, 0)

    def own_x(b, carry):
        cols = pl.multiple_of(b * 512 + core * 256, 256)
        rows = pl.multiple_of(b * 256, 256)
        xt_ref[pl.ds(rows, 256), 0:512] = x_ref[:, pl.ds(cols, 256)].T
        return carry

    lax.fori_loop(0, 8, own_x, 0)

    def got_x(b, carry):
        copy_x(b).wait_recv()
        rows = pl.multiple_of(b * 256, 256)
        xt_ref[pl.ds(rows, 256), 512:1024] = xr[b].astype(BF16).T
        return carry

    lax.fori_loop(0, 8, got_x, 0)
    for h in range(2):
        copy_d(h).wait_recv()
        dvh_ref[h, 512:1024, :] = dr[h].astype(BF16)
    for h in range(2):
        copy_d(h).wait_send()

    def sent_x(b, carry):
        copy_x(b).wait_send()
        return carry

    lax.fori_loop(0, 8, sent_x, 0)


def pair(x, dv):
    return pl.pallas_call(
        pair_kernel,
        out_shape=(
            jax.ShapeDtypeStruct((2048, 1024), BF16),
            jax.ShapeDtypeStruct((2, 1024, 1024), BF16),
        ),
        in_specs=[pl.BlockSpec(memory_space=pltpu.VMEM)] * 2,
        out_specs=(pl.BlockSpec(memory_space=pltpu.VMEM),) * 2,
        scratch_shapes=[
            pltpu.VMEM((8, 512, 256), F32), pltpu.VMEM((8, 512, 256), F32),
            pltpu.VMEM((2, 512, 1024), F32), pltpu.VMEM((2, 512, 1024), F32),
            pltpu.SemaphoreType.DMA((10,)), pltpu.SemaphoreType.DMA((10,)),
        ],
        compiler_params=pltpu.CompilerParams(
            collective_id=2, has_side_effects=True, vmem_limit_bytes=60 << 20
        ),
        name="pair",
    )(x, dv)


def prefix(value, axis, join, neutral, backward):
    count, mine = (lax.axis_size(axis), lax.axis_index(axis))
    pieces = lax.all_gather(value, axis)
    if backward:
        pieces = pieces[::-1]
        mine = count - 1 - mine
    total = jnp.full_like(value, 0) + jnp.asarray(neutral, value.dtype)

    def step(position, total):
        longer = join(total, pieces[position])
        return jnp.where(position < mine, longer, total)

    return lax.fori_loop(0, count - 1, step, total)


def add_states(earlier, later):
    return earlier + later


def per_device(layer_input, queries, key_vectors, value_vectors, grad_output):
    tok_rows = queries.shape[1]
    block_len = min(tok_rows, BLK)
    block_count = tok_rows // block_len

    def split(array):
        return array.reshape(block_count, block_len, H, HDIM)

    q_blocks = split(queries)
    k_blocks = split(key_vectors)
    v_blocks = split(value_vectors)
    g_blocks = split(grad_output)
    kv_sum = jnp.einsum("bthe,bthf->bhef", k_blocks, v_blocks, preferred_element_type=jnp.float32)
    qg_sum = jnp.einsum("bthe,bthf->bhef", q_blocks, g_blocks, preferred_element_type=jnp.float32)
    kv_device = jnp.sum(kv_sum, axis=0)
    qg_device = jnp.sum(qg_sum, axis=0)
    zero_state = jnp.zeros((H, HDIM, HDIM), jnp.float32)
    before_device = prefix(kv_device, "seq", add_states, zero_state, False)
    after_device = prefix(qg_device, "seq", add_states, zero_state, True)
    before = before_device + (jnp.cumsum(kv_sum, axis=0) - kv_sum)
    after = after_device + (qg_device - jnp.cumsum(qg_sum, axis=0))
    before_r = before.astype(jnp.bfloat16)
    after_r = after.astype(jnp.bfloat16)
    causal = jnp.tril(jnp.ones((block_len, block_len), dtype=bool))
    within = jnp.where(
        causal,
        jnp.einsum("bthe,bshe->bhts", q_blocks, k_blocks, preferred_element_type=jnp.float32),
        0.0,
    ).astype(jnp.bfloat16)
    back = jnp.where(
        causal,
        jnp.einsum("bthf,bshf->bhts", g_blocks, v_blocks, preferred_element_type=jnp.float32),
        0.0,
    ).astype(jnp.bfloat16)
    grad_q = jnp.einsum(
        "bhts,bshe->bthe", back, k_blocks, preferred_element_type=jnp.float32
    ) + jnp.einsum("bthf,bhef->bthe", g_blocks, before_r, preferred_element_type=jnp.float32)
    grad_k = jnp.einsum(
        "bhts,bthe->bshe", back, q_blocks, preferred_element_type=jnp.float32
    ) + jnp.einsum("bshf,bhef->bshe", v_blocks, after_r, preferred_element_type=jnp.float32)
    grad_v = jnp.einsum(
        "bhts,bthf->bshf", within, g_blocks, preferred_element_type=jnp.float32
    ) + jnp.einsum("bshe,bhef->bshf", k_blocks, after_r, preferred_element_type=jnp.float32)
    grad_queries = grad_q.astype(jnp.bfloat16).reshape(1, tok_rows, HD)
    grad_keys = grad_k.astype(jnp.bfloat16).reshape(1, tok_rows, HD)
    grad_values = grad_v.astype(jnp.bfloat16).reshape(1, tok_rows, HD)
    input_rows = layer_input[0]
    value_rows = grad_values[0]
    xt, dvh = pair(input_rows, value_rows)
    grad_weight = weight(xt, dvh)
    return (grad_queries, grad_keys, grad_values, grad_weight)


def solution(mesh):
    return jax.shard_map(
        per_device,
        mesh=mesh,
        in_specs=(
            P("grp", "seq", None),
            P("grp", "seq", None),
            P("grp", "seq", None),
            P("grp", "seq", None),
            P("grp", "seq", None),
        ),
        out_specs=(
            P("grp", "seq", None),
            P("grp", "seq", None),
            P("grp", "seq", None),
            P("seq", "grp"),
        ),
        check_vma=False,
    )
```

```python
import jax
import jax.numpy as jnp
from jax import lax
from jax.experimental import pallas as pl
from jax.experimental.pallas import tpu as pltpu
from jax.sharding import PartitionSpec as P

MESH = pl.DeviceIdType.MESH
H = 16
HDIM = 128
BLK = 512
HD = 2048
F32 = jnp.float32
BF16 = jnp.bfloat16

ROWS = {
    (0, 0): (48, 40), (0, 1): (40, 48), (0, 2): (40, 40),
    (1, 0): (40, 48), (1, 1): (48, 40), (1, 2): (40, 40),
}
ORDER = (("x", "y", "z"), ("y", "z", "x"), ("z", "x", "y"))
UNITS = [(h, c, f) for h in range(2) for c in range(3) for f in range(2)]


def row_start(h, c, f):
    start = sum(sum(ROWS[(h, prior)]) for prior in range(c))
    return start + (ROWS[(h, c)][0] if f else 0)


def place():
    seq, grp = lax.axis_index("seq"), lax.axis_index("grp")
    core = lax.rem(seq, 2)
    y_lo = lax.rem(lax.div(seq, 2), 2)
    return {
        "x": lax.rem(grp, 4),
        "y": lax.div(grp, 4) * 2 + y_lo,
        "z": lax.div(seq, 4),
        "core": core,
    }


def device(at):
    return (
        at["z"] * 4 + lax.rem(at["y"], 2) * 2 + at["core"],
        lax.div(at["y"], 2) * 4 + at["x"],
    )


def shifted(at, axis, delta):
    moved = dict(at)
    moved[axis] = lax.rem(at[axis] + delta + 4, 4)
    return device(moved)


def partner_of(at):
    moved = dict(at)
    moved["core"] = 1 - at["core"]
    return device(moved)


def greet(devices):
    barrier = pltpu.get_barrier_semaphore()
    for other in devices:
        pl.semaphore_signal(barrier, inc=1, device_id=other, device_id_type=MESH)
    pl.semaphore_wait(barrier, len(devices))


def weight_kernel(xt_ref, dv_ref, out_ref, *scratch):
    parts = {unit: scratch[4 * i] for i, unit in enumerate(UNITS)}
    landing = {unit: scratch[4 * i + 1 : 4 * i + 4] for i, unit in enumerate(UNITS)}
    send_sem, recv_sem = scratch[4 * len(UNITS) :]
    at = place()
    greet([shifted(at, axis, delta) for axis in "xyz" for delta in (1, -1)])

    def view(unit, stage):
        ref = parts[unit]
        for earlier in range(stage):
            ref = ref.at[at[ORDER[unit[1]][earlier]]]
        return ref

    def hop(unit, stage, kind):
        index = UNITS.index(unit)
        axis = ORDER[unit[1]][stage]
        sign = 1 if unit[2] else -1
        mine = at[axis]
        chunk, toward = (
            (lax.rem(mine + 2, 4), sign),
            (lax.rem(mine - sign + 4, 4), -sign),
            (lax.rem(mine + sign + 4, 4), sign),
        )[kind]
        return pltpu.make_async_remote_copy(
            src_ref=view(unit, stage).at[chunk],
            dst_ref=landing[unit][stage].at[kind],
            send_sem=send_sem.at[index, stage, kind],
            recv_sem=recv_sem.at[index, stage, kind],
            device_id=shifted(at, axis, toward),
            device_id_type=MESH,
        )

    def compute(h):
        def block(b, carry):
            rows = pl.multiple_of(b * 256, 256)
            z, y_lo = lax.div(b, 2), lax.rem(b, 2)
            lhs = xt_ref[pl.ds(rows, 256), :]
            for pair in range(4):
                acc = jnp.dot(
                    lhs,
                    dv_ref[h, :, pair * 256 : pair * 256 + 256],
                    preferred_element_type=F32,
                )
                for side in range(2):
                    tile = 2 * pair + side
                    dest = {"x": tile % 4, "y": (tile // 4) * 2 + y_lo, "z": z}
                    for c in range(3):
                        for f in range(2):
                            start = row_start(h, c, f)
                            i, j, k = (dest[axis] for axis in ORDER[c])
                            parts[(h, c, f)][i, j, k] = acc[
                                start : start + ROWS[(h, c)][f],
                                side * 128 : side * 128 + 128,
                            ]
            return carry

        lax.fori_loop(0, 8, block, 0)

    def units_of(h):
        return [unit for unit in UNITS if unit[0] == h]

    def issue(h, stage):
        for kind in range(2):
            for unit in units_of(h):
                hop(unit, stage, kind).start()

    def combine(h, stage):
        for unit in units_of(h):
            axis = ORDER[unit[1]][stage]
            sign = 1 if unit[2] else -1
            hop(unit, stage, 0).wait_recv()
            target = view(unit, stage).at[lax.rem(at[axis] + sign + 4, 4)]
            arrived = landing[unit][stage].at[0]
            if stage == 0:
                def add(i, carry, target=target, arrived=arrived):
                    target[i] = target[i] + arrived[i]
                    return carry

                lax.fori_loop(0, 4, add, 0)
            else:
                target[...] = target[...] + arrived[...]
            hop(unit, stage, 2).start()

    def final(h, stage, then):
        for unit in units_of(h):
            axis = ORDER[unit[1]][stage]
            hop(unit, stage, 1).wait_recv()
            hop(unit, stage, 2).wait_recv()
            target = view(unit, stage).at[at[axis]]
            direct = landing[unit][stage].at[1]
            summed = landing[unit][stage].at[2]
            if stage == 0:
                def add(i, carry, target=target, direct=direct, summed=summed):
                    target[i] = target[i] + direct[i] + summed[i]
                    return carry

                lax.fori_loop(0, 4, add, 0)
            elif stage == 1:
                target[...] = target[...] + direct[...] + summed[...]
            else:
                start = row_start(*unit)
                total = target[...] + direct[...] + summed[...]
                out_ref[start : start + ROWS[unit[:2]][unit[2]], h * 128 : h * 128 + 128] = (
                    total * SCALE
                )
            if then:
                hop(unit, stage + 1, 0).start()
                hop(unit, stage + 1, 1).start()

    compute(0)
    issue(0, 0)
    compute(1)
    combine(0, 0)
    issue(1, 0)
    final(0, 0, True)
    combine(1, 0)
    combine(0, 1)
    final(0, 1, True)
    final(1, 0, True)
    combine(0, 2)
    final(0, 2, False)
    combine(1, 1)
    final(1, 1, True)
    combine(1, 2)
    final(1, 2, False)
    for unit in UNITS:
        for stage in range(3):
            for kind in range(3):
                hop(unit, stage, kind).wait_send()


SCALE = 65536.0 ** -0.5


def weight(xt, dvh):
    scratch = []
    for h, c, f in UNITS:
        r = ROWS[(h, c)][f]
        scratch.append(pltpu.VMEM((4, 4, 4, r, 128), F32))
        scratch.append(pltpu.VMEM((3, 4, 4, r, 128), F32))
        scratch.append(pltpu.VMEM((3, 4, r, 128), F32))
        scratch.append(pltpu.VMEM((3, r, 128), F32))
    scratch.append(pltpu.SemaphoreType.DMA((len(UNITS), 3, 3)))
    scratch.append(pltpu.SemaphoreType.DMA((len(UNITS), 3, 3)))
    return pl.pallas_call(
        weight_kernel,
        out_shape=jax.ShapeDtypeStruct((256, 256), F32),
        in_specs=[pl.BlockSpec(memory_space=pltpu.VMEM)] * 2,
        out_specs=pl.BlockSpec(memory_space=pltpu.VMEM),
        scratch_shapes=scratch,
        compiler_params=pltpu.CompilerParams(
            collective_id=1, has_side_effects=True, vmem_limit_bytes=60 << 20
        ),
        name="weight_rs",
    )(xt, dvh)


def grads_kernel(
    x_hbm, q_hbm, k_hbm, v_hbm, g_hbm,
    gq_hbm, gk_hbm, gv_hbm, xt_ref, dvh_ref,
    qb, kb, vb, gb, sums, paired, zgot, zsend, ygot, ysend, fgot, fsend, state,
    gq, gk, gv, xb, xs, xr, ds, dr,
    load_sem, xload_sem, out_sem, pair_sems, z_sems, y_sems, f_sems, x_sems, d_sems,
):
    at = place()
    core = at["core"]
    z = at["z"]
    y_lo = lax.rem(at["y"], 2)
    other = partner_of(at)
    beside = dict(at)
    beside["y"] = at["y"] + 1 - 2 * y_lo
    beside = device(beside)

    loads = [
        pltpu.make_async_copy(src, dst, load_sem.at[i])
        for i, (src, dst) in enumerate(
            ((q_hbm, qb), (g_hbm, gb), (k_hbm, kb), (v_hbm, vb))
        )
    ]
    for load in loads:
        load.start()

    def load_x(b):
        cols = pl.multiple_of(b * 512, 512)
        slot = lax.rem(b, 2)
        return pltpu.make_async_copy(
            x_hbm.at[:, pl.ds(cols, 512)], xb.at[slot], xload_sem.at[slot]
        )

    load_x(0).start()
    load_x(1).start()

    def remote(src, dst, sems, index, target):
        send, recv = sems
        for i in index:
            send, recv = send.at[i], recv.at[i]
        return pltpu.make_async_remote_copy(
            src_ref=src, dst_ref=dst, send_sem=send, recv_sem=recv,
            device_id=target, device_id_type=MESH,
        )

    def pair_copy(st, j):
        return remote(sums.at[st, 1 - core, j], paired.at[st, j], pair_sems, (st, j), other)

    def z_copy(st, j):
        return remote(
            zsend.at[st, j], zgot.at[st, j], z_sems, (st, j),
            shifted(at, "z", 1 if st else -1),
        )

    def y_copy(st, j):
        return remote(ysend.at[st, j], ygot.at[st, j], y_sems, (st, j), beside)

    def f_copy(st, j):
        return remote(fsend.at[st, j], fgot.at[st, j], f_sems, (st, j), other)

    def x_copy(b):
        return remote(xs.at[lax.rem(b, 2)], xr.at[b], x_sems, (b,), other)

    def d_copy(head):
        return remote(ds.at[head], dr.at[head], d_sems, (head,), other)

    for st in range(2):
        @pl.when(z == (0 if st else 3))
        def _(st=st):
            zgot[st] = jnp.zeros((8, HDIM, HDIM), F32)

    greet([other, beside, shifted(at, "z", 1), shifted(at, "z", -1)])

    def lanes(head):
        return pl.ds(pl.multiple_of(head * HDIM, HDIM), HDIM)

    def outer(lhs, rhs, head):
        return lax.dot_general(
            lhs[:, lanes(head)], rhs[:, lanes(head)], (((0,), (0,)), ((), ())),
            preferred_element_type=F32,
        )

    def sum_states(st, lhs, rhs):
        def theirs(j, carry):
            sums[st, 1 - core, j] = outer(lhs, rhs, (1 - core) * 8 + j)
            pair_copy(st, j).start()
            return carry

        def mine(j, carry):
            sums[st, core, j] = outer(lhs, rhs, core * 8 + j)
            return carry

        lax.fori_loop(0, 8, theirs, 0)
        lax.fori_loop(0, 8, mine, 0)

    loads[0].wait()
    loads[1].wait()
    sum_states(0, qb, gb)
    loads[2].wait()
    loads[3].wait()
    sum_states(1, kb, vb)

    def chain(st, j):
        pair_copy(st, j).wait_recv()

        @pl.when(z != (0 if st else 3))
        def _():
            z_copy(st, j).wait_recv()

        chip = sums[st, core, j] + paired[st, j]
        far = zgot[st, j]
        zsend[st, j] = chip + far
        full = y_lo == (0 if st else 1)
        ysend[st, j] = far + jnp.where(full, chip, 0.0)

        @pl.when(z != (3 if st else 0))
        def _():
            z_copy(st, j).start()

        y_copy(st, j).start()

    def settle(st, j):
        y_copy(st, j).wait_recv()
        both = zgot[st, j] + ygot[st, j]
        inner = 1 if st else 0
        fsend[st, j] = both + jnp.where(core != inner, sums[st, core, j], 0.0)
        f_copy(st, j).start()
        state[st, core * 8 + j] = (
            both + jnp.where(core == inner, paired[st, j], 0.0)
        ).astype(BF16)

    def receive(st, j):
        f_copy(st, j).wait_recv()
        state[st, (1 - core) * 8 + j] = fgot[st, j].astype(BF16)

    def nt(lhs, rhs):
        return lax.dot_general(lhs, rhs, (((1,), (1,)), ((), ())), preferred_element_type=F32)

    def nn(lhs, rhs):
        return jnp.dot(lhs, rhs, preferred_element_type=F32)

    half = 256
    row = lax.broadcasted_iota(jnp.int32, (half, half), 0)
    col = lax.broadcasted_iota(jnp.int32, (half, half), 1)

    def lower(block):
        return jnp.where(col <= row, block, 0.0).astype(BF16)

    def upper(block):
        return jnp.where(row <= col, block, 0.0).astype(BF16)

    def local(head):
        q, k = qb[:, lanes(head)], kb[:, lanes(head)]
        v, g = vb[:, lanes(head)], gb[:, lanes(head)]
        q0, q1, k0, k1 = q[:half], q[half:], k[:half], k[half:]
        v0, v1, g0, g1 = v[:half], v[half:], g[:half], g[half:]
        gv[head, 0:half] = nn(upper(nt(k0, q0)), g0) + nn(nt(k0, q1).astype(BF16), g1)
        gv[head, half:BLK] = nn(upper(nt(k1, q1)), g1)
        gk[head, 0:half] = nn(upper(nt(v0, g0)), q0) + nn(nt(v0, g1).astype(BF16), q1)
        gk[head, half:BLK] = nn(upper(nt(v1, g1)), q1)
        gq[head, 0:half] = nn(lower(nt(g0, v0)), k0)
        gq[head, half:BLK] = nn(nt(g1, v0).astype(BF16), k0) + nn(lower(nt(g1, v1)), k1)

    def send_x(b):
        slot = lax.rem(b, 2)
        load_x(b).wait()

        @pl.when(b >= 2)
        def _():
            x_copy(b - 2).wait_send()

        theirs = pl.multiple_of((1 - core) * 256, 256)
        mine = pl.multiple_of(core * 256, 256)
        xs[slot] = xb[slot, :, pl.ds(theirs, 256)].astype(F32)
        x_copy(b).start()
        rows = pl.multiple_of(b * 256, 256)
        xt_ref[pl.ds(rows, 256), 0:BLK] = xb[slot, :, pl.ds(mine, 256)].T

        @pl.when(b < 6)
        def _():
            load_x(b + 2).start()

    def take_x(b):
        x_copy(b).wait_recv()
        rows = pl.multiple_of(b * 256, 256)
        xt_ref[pl.ds(rows, 256), BLK : 2 * BLK] = xr[b].astype(BF16).T

    LAG = 3

    def slot_step(i, carry):
        for st in range(2):
            first = LAG * (z if st else 3 - z)
            j = i - first

            @pl.when(jnp.logical_and(j >= 0, j < 8))
            def _(st=st, j=j):
                chain(st, j)

            @pl.when(jnp.logical_and(j >= LAG, j < 8 + LAG))
            def _(st=st, j=j):
                settle(st, j - LAG)

        @pl.when(i < 8)
        def _():
            send_x(i)

        @pl.when(jnp.logical_and(i >= 8, i < 16))
        def _():
            take_x(i - 8)

        @pl.when(i < 16)
        def _():
            local(i)

        return carry

    lax.fori_loop(0, 8 + 4 * LAG, slot_step, 0)

    def each(count, body):
        def run(i, carry):
            body(i)
            return carry

        lax.fori_loop(0, count, run, 0)

    each(8, lambda j: receive(0, j))

    def finish_v(head):
        total = gv[head] + nn(kb[:, lanes(head)], state[0, head])
        rounded = total.astype(BF16)
        ds[head] = rounded.astype(F32)
        d_copy(head).start()
        kb[:, lanes(head)] = rounded
        h, place_in = lax.rem(head, 2), lax.div(head, 2)
        dvh_ref[h, 0:BLK, lanes(place_in)] = rounded

    each(16, finish_v)
    stores = [
        pltpu.make_async_copy(src, dst, out_sem.at[i])
        for i, (src, dst) in enumerate(((gb, gq_hbm), (vb, gk_hbm), (kb, gv_hbm)))
    ]
    stores[2].start()

    def finish_k(head):
        total = gk[head] + nt(vb[:, lanes(head)], state[0, head])
        vb[:, lanes(head)] = total.astype(BF16)

    each(16, finish_k)
    stores[1].start()
    each(8, lambda j: receive(1, j))

    def finish_q(head):
        total = gq[head] + nt(gb[:, lanes(head)], state[1, head])
        gb[:, lanes(head)] = total.astype(BF16)

    each(16, finish_q)
    stores[0].start()

    def take_d(head):
        d_copy(head).wait_recv()
        h, place_in = lax.rem(head, 2), lax.div(head, 2)
        dvh_ref[h, BLK : 2 * BLK, lanes(place_in)] = dr[head].astype(BF16)

    each(16, take_d)
    each(16, lambda head: d_copy(head).wait_send())
    each(2, lambda b: x_copy(b + 6).wait_send())
    for st in range(2):
        def drain(j, st=st):
            pair_copy(st, j).wait_send()
            y_copy(st, j).wait_send()
            f_copy(st, j).wait_send()

            @pl.when(z != (3 if st else 0))
            def _():
                z_copy(st, j).wait_send()

        each(8, drain)
    for store in stores:
        store.wait()


def grads(x, q, k, v, g):
    wide = jax.ShapeDtypeStruct((BLK, HD), BF16)
    dma = pltpu.SemaphoreType.DMA
    hop = pltpu.VMEM((2, 8, HDIM, HDIM), F32)
    partial = pltpu.VMEM((H, BLK, HDIM), F32)
    any_spec = pl.BlockSpec(memory_space=pl.ANY)
    vmem_spec = pl.BlockSpec(memory_space=pltpu.VMEM)
    return pl.pallas_call(
        grads_kernel,
        out_shape=(
            wide, wide, wide,
            jax.ShapeDtypeStruct((2048, 1024), BF16),
            jax.ShapeDtypeStruct((2, 1024, 1024), BF16),
        ),
        in_specs=[any_spec] * 5,
        out_specs=(any_spec,) * 3 + (vmem_spec,) * 2,
        scratch_shapes=[
            *[pltpu.VMEM((BLK, HD), BF16)] * 4,
            pltpu.VMEM((2, 2, 8, HDIM, HDIM), F32),
            *[hop] * 7,
            pltpu.VMEM((2, H, HDIM, HDIM), BF16),
            *[partial] * 3,
            pltpu.VMEM((2, BLK, 512), BF16),
            pltpu.VMEM((2, BLK, 256), F32),
            pltpu.VMEM((8, BLK, 256), F32),
            partial, partial,
            dma((4,)), dma((2,)), dma((3,)),
            *[(dma((2, 8)), dma((2, 8)))] * 4,
            (dma((8,)), dma((8,))),
            (dma((H,)), dma((H,))),
        ],
        compiler_params=pltpu.CompilerParams(
            collective_id=2, has_side_effects=True, vmem_limit_bytes=62 << 20
        ),
        name="grads",
    )(x, q, k, v, g)


def per_device(layer_input, queries, key_vectors, value_vectors, grad_output):
    arrays = (layer_input, queries, key_vectors, value_vectors, grad_output)
    gq, gk, gv, xt, dvh = grads(*(array[0] for array in arrays))
    grad_weight = weight(xt, dvh)
    return (gq[None], gk[None], gv[None], grad_weight)


def solution(mesh):
    return jax.shard_map(
        per_device,
        mesh=mesh,
        in_specs=(
            P("grp", "seq", None),
            P("grp", "seq", None),
            P("grp", "seq", None),
            P("grp", "seq", None),
            P("grp", "seq", None),
        ),
        out_specs=(
            P("grp", "seq", None),
            P("grp", "seq", None),
            P("grp", "seq", None),
            P("seq", "grp"),
        ),
        check_vma=False,
    )
```

```python
import jax
import jax.numpy as jnp
from jax import lax
from jax.experimental import pallas as pl
from jax.experimental.pallas import tpu as pltpu
from jax.sharding import PartitionSpec as P

MESH = pl.DeviceIdType.MESH
H = 16
HDIM = 128
BLK = 512
HD = 2048
F32 = jnp.float32
BF16 = jnp.bfloat16

ROWS = {
    (0, 0): (48, 40), (0, 1): (40, 48), (0, 2): (40, 40),
    (1, 0): (40, 48), (1, 1): (48, 40), (1, 2): (40, 40),
}
ORDER = (("x", "y", "z"), ("y", "z", "x"), ("z", "x", "y"))
UNITS = [(h, c, f) for h in range(2) for c in range(3) for f in range(2)]


def row_start(h, c, f):
    start = sum(sum(ROWS[(h, prior)]) for prior in range(c))
    return start + (ROWS[(h, c)][0] if f else 0)


def place():
    seq, grp = lax.axis_index("seq"), lax.axis_index("grp")
    core = lax.rem(seq, 2)
    y_lo = lax.rem(lax.div(seq, 2), 2)
    return {
        "x": lax.rem(grp, 4),
        "y": lax.div(grp, 4) * 2 + y_lo,
        "z": lax.div(seq, 4),
        "core": core,
    }


def device(at):
    return (
        at["z"] * 4 + lax.rem(at["y"], 2) * 2 + at["core"],
        lax.div(at["y"], 2) * 4 + at["x"],
    )


def shifted(at, axis, delta):
    moved = dict(at)
    moved[axis] = lax.rem(at[axis] + delta + 4, 4)
    return device(moved)


def partner_of(at):
    moved = dict(at)
    moved["core"] = 1 - at["core"]
    return device(moved)


def greet(devices):
    barrier = pltpu.get_barrier_semaphore()
    for other in devices:
        pl.semaphore_signal(barrier, inc=1, device_id=other, device_id_type=MESH)
    pl.semaphore_wait(barrier, len(devices))


def lanes(head):
    return pl.ds(pl.multiple_of(head * HDIM, HDIM), HDIM)


def nt(lhs, rhs):
    return lax.dot_general(lhs, rhs, (((1,), (1,)), ((), ())), preferred_element_type=F32)


def nn(lhs, rhs):
    return jnp.dot(lhs, rhs, preferred_element_type=F32)


HALF = BLK // 2


def lower(block):
    row = lax.broadcasted_iota(jnp.int32, (HALF, HALF), 0)
    col = lax.broadcasted_iota(jnp.int32, (HALF, HALF), 1)
    return jnp.where(col <= row, block, 0.0).astype(BF16)


def upper(block):
    row = lax.broadcasted_iota(jnp.int32, (HALF, HALF), 0)
    col = lax.broadcasted_iota(jnp.int32, (HALF, HALF), 1)
    return jnp.where(row <= col, block, 0.0).astype(BF16)


def weight_kernel(
    xt_ref, dv_ref, state_ref, q_hbm, k_hbm, v_hbm, g_hbm,
    out_ref, gq_hbm, gk_hbm, qb, kb, vb, gb, load_sem, store_sem, *scratch
):
    loads = [
        pltpu.make_async_copy(src, dst, load_sem.at[i])
        for i, (src, dst) in enumerate(
            ((q_hbm, qb), (k_hbm, kb), (v_hbm, vb), (g_hbm, gb))
        )
    ]
    for load in loads:
        load.start()
    parts = {unit: scratch[4 * i] for i, unit in enumerate(UNITS)}
    landing = {unit: scratch[4 * i + 1 : 4 * i + 4] for i, unit in enumerate(UNITS)}
    send_sem, recv_sem = scratch[4 * len(UNITS) :]
    at = place()
    greet([shifted(at, axis, delta) for axis in "xyz" for delta in (1, -1)])

    def view(unit, stage):
        ref = parts[unit]
        for earlier in range(stage):
            ref = ref.at[at[ORDER[unit[1]][earlier]]]
        return ref

    def hop(unit, stage, kind):
        index = UNITS.index(unit)
        axis = ORDER[unit[1]][stage]
        sign = 1 if unit[2] else -1
        mine = at[axis]
        chunk, toward = (
            (lax.rem(mine + 2, 4), sign),
            (lax.rem(mine - sign + 4, 4), -sign),
            (lax.rem(mine + sign + 4, 4), sign),
        )[kind]
        return pltpu.make_async_remote_copy(
            src_ref=view(unit, stage).at[chunk],
            dst_ref=landing[unit][stage].at[kind],
            send_sem=send_sem.at[index, stage, kind],
            recv_sem=recv_sem.at[index, stage, kind],
            device_id=shifted(at, axis, toward),
            device_id_type=MESH,
        )

    def compute(h):
        def block(b, carry):
            rows = pl.multiple_of(b * 256, 256)
            z, y_lo = lax.div(b, 2), lax.rem(b, 2)
            lhs = xt_ref[pl.ds(rows, 256), :]
            for pair in range(4):
                acc = jnp.dot(
                    lhs,
                    dv_ref[h, :, pair * 256 : pair * 256 + 256],
                    preferred_element_type=F32,
                )
                for side in range(2):
                    tile = 2 * pair + side
                    dest = {"x": tile % 4, "y": (tile // 4) * 2 + y_lo, "z": z}
                    for c in range(3):
                        for f in range(2):
                            start = row_start(h, c, f)
                            i, j, k = (dest[axis] for axis in ORDER[c])
                            parts[(h, c, f)][i, j, k] = acc[
                                start : start + ROWS[(h, c)][f],
                                side * 128 : side * 128 + 128,
                            ]
            return carry

        lax.fori_loop(0, 8, block, 0)

    def units_of(h):
        return [unit for unit in UNITS if unit[0] == h]

    def issue(h, stage):
        for kind in range(2):
            for unit in units_of(h):
                hop(unit, stage, kind).start()

    def combine(h, stage):
        for unit in units_of(h):
            axis = ORDER[unit[1]][stage]
            sign = 1 if unit[2] else -1
            hop(unit, stage, 0).wait_recv()
            target = view(unit, stage).at[lax.rem(at[axis] + sign + 4, 4)]
            arrived = landing[unit][stage].at[0]
            if stage == 0:
                def add(i, carry, target=target, arrived=arrived):
                    target[i] = target[i] + arrived[i]
                    return carry

                lax.fori_loop(0, 4, add, 0)
            else:
                target[...] = target[...] + arrived[...]
            hop(unit, stage, 2).start()

    def final(h, stage, then):
        for unit in units_of(h):
            axis = ORDER[unit[1]][stage]
            hop(unit, stage, 1).wait_recv()
            hop(unit, stage, 2).wait_recv()
            target = view(unit, stage).at[at[axis]]
            direct = landing[unit][stage].at[1]
            summed = landing[unit][stage].at[2]
            if stage == 0:
                def add(i, carry, target=target, direct=direct, summed=summed):
                    target[i] = target[i] + direct[i] + summed[i]
                    return carry

                lax.fori_loop(0, 4, add, 0)
            elif stage == 1:
                target[...] = target[...] + direct[...] + summed[...]
            else:
                start = row_start(*unit)
                total = target[...] + direct[...] + summed[...]
                out_ref[start : start + ROWS[unit[:2]][unit[2]], h * 128 : h * 128 + 128] = (
                    total * SCALE
                )
            if then:
                hop(unit, stage + 1, 0).start()
                hop(unit, stage + 1, 1).start()

    def attend(head):
        q, k = qb[:, lanes(head)], kb[:, lanes(head)]
        v, g = vb[:, lanes(head)], gb[:, lanes(head)]
        q0, q1, k0, k1 = q[:HALF], q[HALF:], k[:HALF], k[HALF:]
        v0, v1, g0, g1 = v[:HALF], v[HALF:], g[:HALF], g[HALF:]
        after, before = state_ref[0, head], state_ref[1, head]
        gk0 = nn(upper(nt(v0, g0)), q0) + nn(nt(v0, g1).astype(BF16), q1) + nt(v0, after)
        gk1 = nn(upper(nt(v1, g1)), q1) + nt(v1, after)
        gq0 = nn(lower(nt(g0, v0)), k0) + nt(g0, before)
        gq1 = (
            nn(nt(g1, v0).astype(BF16), k0) + nn(lower(nt(g1, v1)), k1) + nt(g1, before)
        )
        vb[0:HALF, lanes(head)] = gk0.astype(BF16)
        vb[HALF:BLK, lanes(head)] = gk1.astype(BF16)
        gb[0:HALF, lanes(head)] = gq0.astype(BF16)
        gb[HALF:BLK, lanes(head)] = gq1.astype(BF16)

    def fill(first, last):
        def run(head, carry):
            attend(head)
            return carry

        lax.fori_loop(first, last, run, 0)

    compute(0)
    issue(0, 0)
    compute(1)
    combine(0, 0)
    issue(1, 0)
    for load in loads:
        load.wait()
    fill(0, 6)
    final(0, 0, True)
    fill(6, 10)
    combine(1, 0)
    fill(10, 13)
    combine(0, 1)
    fill(13, 16)
    stores = [
        pltpu.make_async_copy(gb, gq_hbm, store_sem.at[0]),
        pltpu.make_async_copy(vb, gk_hbm, store_sem.at[1]),
    ]
    for store in stores:
        store.start()
    final(0, 1, True)
    final(1, 0, True)
    combine(0, 2)
    final(0, 2, False)
    combine(1, 1)
    final(1, 1, True)
    combine(1, 2)
    final(1, 2, False)
    for unit in UNITS:
        for stage in range(3):
            for kind in range(3):
                hop(unit, stage, kind).wait_send()
    for store in stores:
        store.wait()


SCALE = 65536.0 ** -0.5


def weight(xt, dvh, state, q, k, v, g):
    wide = jax.ShapeDtypeStruct((BLK, HD), BF16)
    any_spec = pl.BlockSpec(memory_space=pl.ANY)
    vmem_spec = pl.BlockSpec(memory_space=pltpu.VMEM)
    scratch = [pltpu.VMEM((BLK, HD), BF16)] * 4
    scratch.append(pltpu.SemaphoreType.DMA((4,)))
    scratch.append(pltpu.SemaphoreType.DMA((2,)))
    for h, c, f in UNITS:
        r = ROWS[(h, c)][f]
        scratch.append(pltpu.VMEM((4, 4, 4, r, 128), F32))
        scratch.append(pltpu.VMEM((3, 4, 4, r, 128), F32))
        scratch.append(pltpu.VMEM((3, 4, r, 128), F32))
        scratch.append(pltpu.VMEM((3, r, 128), F32))
    scratch.append(pltpu.SemaphoreType.DMA((len(UNITS), 3, 3)))
    scratch.append(pltpu.SemaphoreType.DMA((len(UNITS), 3, 3)))
    return pl.pallas_call(
        weight_kernel,
        out_shape=(jax.ShapeDtypeStruct((256, 256), F32), wide, wide),
        in_specs=[vmem_spec] * 3 + [any_spec] * 4,
        out_specs=(vmem_spec, any_spec, any_spec),
        scratch_shapes=scratch,
        compiler_params=pltpu.CompilerParams(
            collective_id=1, has_side_effects=True, vmem_limit_bytes=60 << 20
        ),
        name="weight_rs",
    )(xt, dvh, state, q, k, v, g)


def grads_kernel(
    x_hbm, q_hbm, k_hbm, v_hbm, g_hbm,
    gv_hbm, xt_ref, dvh_ref, state,
    qb, kb, vb, gb, sums, paired, zgot, zsend, ygot, ysend, fgot, fsend,
    gv, xb, xs, xr, ds, dr,
    load_sem, xload_sem, out_sem, pair_sems, z_sems, y_sems, f_sems, x_sems, d_sems,
):
    at = place()
    core = at["core"]
    z = at["z"]
    y_lo = lax.rem(at["y"], 2)
    other = partner_of(at)
    beside = dict(at)
    beside["y"] = at["y"] + 1 - 2 * y_lo
    beside = device(beside)

    loads = [
        pltpu.make_async_copy(src, dst, load_sem.at[i])
        for i, (src, dst) in enumerate(
            ((q_hbm, qb), (g_hbm, gb), (k_hbm, kb), (v_hbm, vb))
        )
    ]
    for load in loads:
        load.start()

    def load_x(b):
        cols = pl.multiple_of(b * 512, 512)
        slot = lax.rem(b, 2)
        return pltpu.make_async_copy(
            x_hbm.at[:, pl.ds(cols, 512)], xb.at[slot], xload_sem.at[slot]
        )

    load_x(0).start()
    load_x(1).start()

    def remote(src, dst, sems, index, target):
        send, recv = sems
        for i in index:
            send, recv = send.at[i], recv.at[i]
        return pltpu.make_async_remote_copy(
            src_ref=src, dst_ref=dst, send_sem=send, recv_sem=recv,
            device_id=target, device_id_type=MESH,
        )

    def pair_copy(st, j):
        return remote(sums.at[st, 1 - core, j], paired.at[st, j], pair_sems, (st, j), other)

    def z_copy(st, j):
        return remote(
            zsend.at[st, j], zgot.at[st, j], z_sems, (st, j),
            shifted(at, "z", 1 if st else -1),
        )

    def y_copy(st, j):
        return remote(ysend.at[st, j], ygot.at[st, j], y_sems, (st, j), beside)

    def f_copy(st, j):
        return remote(fsend.at[st, j], fgot.at[st, j], f_sems, (st, j), other)

    def x_copy(b):
        return remote(xs.at[lax.rem(b, 2)], xr.at[b], x_sems, (b,), other)

    def d_copy(head):
        return remote(ds.at[head], dr.at[head], d_sems, (head,), other)

    for st in range(2):
        @pl.when(z == (0 if st else 3))
        def _(st=st):
            zgot[st] = jnp.zeros((8, HDIM, HDIM), F32)

    greet([other, beside, shifted(at, "z", 1), shifted(at, "z", -1)])

    def outer(lhs, rhs, head):
        return lax.dot_general(
            lhs[:, lanes(head)], rhs[:, lanes(head)], (((0,), (0,)), ((), ())),
            preferred_element_type=F32,
        )

    loads[0].wait()
    loads[1].wait()

    def theirs(j, carry):
        sums[0, 1 - core, j] = outer(qb, gb, (1 - core) * 8 + j)
        pair_copy(0, j).start()
        return carry

    def mine(j, carry):
        sums[0, core, j] = outer(qb, gb, core * 8 + j)
        return carry

    lax.fori_loop(0, 8, theirs, 0)
    lax.fori_loop(0, 8, mine, 0)
    loads[2].wait()
    loads[3].wait()

    def sum_keys(j):
        sums[1, 1 - core, j] = outer(kb, vb, (1 - core) * 8 + j)
        pair_copy(1, j).start()
        sums[1, core, j] = outer(kb, vb, core * 8 + j)

    def chain(st, j):
        pair_copy(st, j).wait_recv()

        @pl.when(z != (0 if st else 3))
        def _():
            z_copy(st, j).wait_recv()

        chip = sums[st, core, j] + paired[st, j]
        far = zgot[st, j]
        zsend[st, j] = chip + far
        full = y_lo == (0 if st else 1)
        ysend[st, j] = far + jnp.where(full, chip, 0.0)

        @pl.when(z != (3 if st else 0))
        def _():
            z_copy(st, j).start()

        y_copy(st, j).start()

    def settle(st, j):
        y_copy(st, j).wait_recv()
        both = zgot[st, j] + ygot[st, j]
        inner = 1 if st else 0
        fsend[st, j] = both + jnp.where(core != inner, sums[st, core, j], 0.0)
        f_copy(st, j).start()
        state[st, core * 8 + j] = (
            both + jnp.where(core == inner, paired[st, j], 0.0)
        ).astype(BF16)

    def receive(st, j):
        f_copy(st, j).wait_recv()
        state[st, (1 - core) * 8 + j] = fgot[st, j].astype(BF16)

    def local(head):
        q, k, g = qb[:, lanes(head)], kb[:, lanes(head)], gb[:, lanes(head)]
        q0, q1, k0, k1 = q[:HALF], q[HALF:], k[:HALF], k[HALF:]
        g0, g1 = g[:HALF], g[HALF:]
        gv[head, 0:HALF] = nn(upper(nt(k0, q0)), g0) + nn(nt(k0, q1).astype(BF16), g1)
        gv[head, HALF:BLK] = nn(upper(nt(k1, q1)), g1)

    def finish_v(head):
        total = gv[head] + nn(kb[:, lanes(head)], state[0, head])
        rounded = total.astype(BF16)
        ds[head] = rounded.astype(F32)
        d_copy(head).start()
        kb[:, lanes(head)] = rounded
        h, place_in = lax.rem(head, 2), lax.div(head, 2)
        dvh_ref[h, 0:BLK, lanes(place_in)] = rounded

    def send_x(b):
        slot = lax.rem(b, 2)
        load_x(b).wait()

        @pl.when(b >= 2)
        def _():
            x_copy(b - 2).wait_send()

        theirs = pl.multiple_of((1 - core) * 256, 256)
        mine = pl.multiple_of(core * 256, 256)
        xs[slot] = xb[slot, :, pl.ds(theirs, 256)].astype(F32)
        x_copy(b).start()
        rows = pl.multiple_of(b * 256, 256)
        xt_ref[pl.ds(rows, 256), 0:BLK] = xb[slot, :, pl.ds(mine, 256)].T

        @pl.when(b < 6)
        def _():
            load_x(b + 2).start()

    def take_x(b):
        x_copy(b).wait_recv()
        rows = pl.multiple_of(b * 256, 256)
        xt_ref[pl.ds(rows, 256), BLK : 2 * BLK] = xr[b].astype(BF16).T

    LAG = 3
    BEHIND = 2

    def slot_step(i, carry):
        def step(st, delay, body):
            j = i - LAG * (z if st else 3 - z) - (BEHIND if st else 0) - delay

            @pl.when(jnp.logical_and(j >= 0, j < 8))
            def _():
                body(j)

        def settled(j):
            settle(0, j)
            finish_v(core * 8 + j)

        def received(j):
            receive(0, j)
            finish_v((1 - core) * 8 + j)

        step(0, 0, lambda j: chain(0, j))
        step(0, LAG, settled)
        step(0, LAG + 1, received)

        @pl.when(i < 8)
        def _():
            sum_keys(i)

        step(1, 0, lambda j: chain(1, j))
        step(1, LAG, lambda j: settle(1, j))

        @pl.when(i < 8)
        def _():
            send_x(i)
            local(core * 8 + i)
            local((1 - core) * 8 + i)

        @pl.when(jnp.logical_and(i >= 8, i < 16))
        def _():
            take_x(i - 8)

        return carry

    lax.fori_loop(0, 8 + 4 * LAG + BEHIND, slot_step, 0)

    def each(count, body):
        def run(i, carry):
            body(i)
            return carry

        lax.fori_loop(0, count, run, 0)

    store = pltpu.make_async_copy(kb, gv_hbm, out_sem.at[0])
    store.start()
    each(8, lambda j: receive(1, j))

    def take_d(head):
        d_copy(head).wait_recv()
        h, place_in = lax.rem(head, 2), lax.div(head, 2)
        dvh_ref[h, BLK : 2 * BLK, lanes(place_in)] = dr[head].astype(BF16)

    each(16, take_d)
    each(16, lambda head: d_copy(head).wait_send())
    each(2, lambda b: x_copy(b + 6).wait_send())
    for st in range(2):
        def drain(j, st=st):
            pair_copy(st, j).wait_send()
            y_copy(st, j).wait_send()
            f_copy(st, j).wait_send()

            @pl.when(z != (3 if st else 0))
            def _():
                z_copy(st, j).wait_send()

        each(8, drain)
    store.wait()


def grads(x, q, k, v, g):
    wide = jax.ShapeDtypeStruct((BLK, HD), BF16)
    dma = pltpu.SemaphoreType.DMA
    hop = pltpu.VMEM((2, 8, HDIM, HDIM), F32)
    partial = pltpu.VMEM((H, BLK, HDIM), F32)
    any_spec = pl.BlockSpec(memory_space=pl.ANY)
    vmem_spec = pl.BlockSpec(memory_space=pltpu.VMEM)
    return pl.pallas_call(
        grads_kernel,
        out_shape=(
            wide,
            jax.ShapeDtypeStruct((2048, 1024), BF16),
            jax.ShapeDtypeStruct((2, 1024, 1024), BF16),
            jax.ShapeDtypeStruct((2, H, HDIM, HDIM), BF16),
        ),
        in_specs=[any_spec] * 5,
        out_specs=(any_spec,) + (vmem_spec,) * 3,
        scratch_shapes=[
            *[pltpu.VMEM((BLK, HD), BF16)] * 4,
            pltpu.VMEM((2, 2, 8, HDIM, HDIM), F32),
            *[hop] * 7,
            partial,
            pltpu.VMEM((2, BLK, 512), BF16),
            pltpu.VMEM((2, BLK, 256), F32),
            pltpu.VMEM((8, BLK, 256), F32),
            partial, partial,
            dma((4,)), dma((2,)), dma((1,)),
            *[(dma((2, 8)), dma((2, 8)))] * 4,
            (dma((8,)), dma((8,))),
            (dma((H,)), dma((H,))),
        ],
        compiler_params=pltpu.CompilerParams(
            collective_id=2, has_side_effects=True, vmem_limit_bytes=62 << 20
        ),
        name="grads",
    )(x, q, k, v, g)


def per_device(layer_input, queries, key_vectors, value_vectors, grad_output):
    arrays = (layer_input, queries, key_vectors, value_vectors, grad_output)
    x, q, k, v, g = (array[0] for array in arrays)
    gv, xt, dvh, state = grads(x, q, k, v, g)
    grad_weight, gq, gk = weight(xt, dvh, state, q, k, v, g)
    return (gq[None], gk[None], gv[None], grad_weight)


def solution(mesh):
    return jax.shard_map(
        per_device,
        mesh=mesh,
        in_specs=(
            P("grp", "seq", None),
            P("grp", "seq", None),
            P("grp", "seq", None),
            P("grp", "seq", None),
            P("grp", "seq", None),
        ),
        out_specs=(
            P("grp", "seq", None),
            P("grp", "seq", None),
            P("grp", "seq", None),
            P("seq", "grp"),
        ),
        check_vma=False,
    )
```

```python
import jax
import jax.numpy as jnp
from jax import lax
from jax.experimental import pallas as pl
from jax.experimental.pallas import tpu as pltpu
from jax.sharding import PartitionSpec as P

MESH = pl.DeviceIdType.MESH
H = 16
HDIM = 128
BLK = 512
HD = 2048
F32 = jnp.float32
BF16 = jnp.bfloat16

ROWS = {
    (0, 0): (48, 40), (0, 1): (40, 48), (0, 2): (40, 40),
    (1, 0): (40, 48), (1, 1): (48, 40), (1, 2): (40, 40),
}
ORDER = (("x", "y", "z"), ("y", "z", "x"), ("z", "x", "y"))
UNITS = [(h, c, f) for h in range(2) for c in range(3) for f in range(2)]


def row_start(h, c, f):
    start = sum(sum(ROWS[(h, prior)]) for prior in range(c))
    return start + (ROWS[(h, c)][0] if f else 0)


def place():
    seq, grp = lax.axis_index("seq"), lax.axis_index("grp")
    core = lax.rem(seq, 2)
    y_lo = lax.rem(lax.div(seq, 2), 2)
    return {
        "x": lax.rem(grp, 4),
        "y": lax.div(grp, 4) * 2 + y_lo,
        "z": lax.div(seq, 4),
        "core": core,
    }


def device(at):
    return (
        at["z"] * 4 + lax.rem(at["y"], 2) * 2 + at["core"],
        lax.div(at["y"], 2) * 4 + at["x"],
    )


def shifted(at, axis, delta):
    moved = dict(at)
    moved[axis] = lax.rem(at[axis] + delta + 4, 4)
    return device(moved)


def partner_of(at):
    moved = dict(at)
    moved["core"] = 1 - at["core"]
    return device(moved)


def greet(devices):
    barrier = pltpu.get_barrier_semaphore()
    for other in devices:
        pl.semaphore_signal(barrier, inc=1, device_id=other, device_id_type=MESH)
    pl.semaphore_wait(barrier, len(devices))


def lanes(head):
    return pl.ds(pl.multiple_of(head * HDIM, HDIM), HDIM)


def nt(lhs, rhs):
    return lax.dot_general(lhs, rhs, (((1,), (1,)), ((), ())), preferred_element_type=F32)


def nn(lhs, rhs):
    return jnp.dot(lhs, rhs, preferred_element_type=F32)


HALF = BLK // 2


def lower(block):
    row = lax.broadcasted_iota(jnp.int32, (HALF, HALF), 0)
    col = lax.broadcasted_iota(jnp.int32, (HALF, HALF), 1)
    return jnp.where(col <= row, block, 0.0).astype(BF16)


def upper(block):
    row = lax.broadcasted_iota(jnp.int32, (HALF, HALF), 0)
    col = lax.broadcasted_iota(jnp.int32, (HALF, HALF), 1)
    return jnp.where(row <= col, block, 0.0).astype(BF16)


def kernel(
    x_hbm, q_hbm, k_hbm, v_hbm, g_hbm,
    gq_hbm, gk_hbm, gv_hbm, out_ref,
    qb, kb, vb, gb, xt_ref, dvh_ref, state,
    sums, paired, zgot, zsend, ygot, ysend, fgot, fsend, xb, xs, tiles,
    load_sem, xload_sem, out_sem, store_sem,
    pair_send, pair_recv, z_send, z_recv, y_send, y_recv, f_send, f_recv,
    x_send, x_recv, d_send, d_recv, *landing_refs
):
    pair_sems, z_sems, y_sems = (pair_send, pair_recv), (z_send, z_recv), (y_send, y_recv)
    f_sems, x_sems, d_sems = (f_send, f_recv), (x_send, x_recv), (d_send, d_recv)
    at = place()
    core = at["core"]
    z = at["z"]
    y_lo = lax.rem(at["y"], 2)
    other = partner_of(at)
    beside = dict(at)
    beside["y"] = at["y"] + 1 - 2 * y_lo
    beside = device(beside)

    loads = [
        pltpu.make_async_copy(src, dst, load_sem.at[i])
        for i, (src, dst) in enumerate(
            ((q_hbm, qb), (g_hbm, gb), (k_hbm, kb), (v_hbm, vb))
        )
    ]
    for load in loads:
        load.start()

    def load_x(b):
        cols = pl.multiple_of(b * 512, 512)
        slot = lax.rem(b, 2)
        return pltpu.make_async_copy(
            x_hbm.at[:, pl.ds(cols, 512)], xb.at[slot], xload_sem.at[slot]
        )

    load_x(0).start()
    load_x(1).start()

    def remote(src, dst, sems, index, target):
        send, recv = sems
        for i in index:
            send, recv = send.at[i], recv.at[i]
        return pltpu.make_async_remote_copy(
            src_ref=src, dst_ref=dst, send_sem=send, recv_sem=recv,
            device_id=target, device_id_type=MESH,
        )

    def pair_copy(st, j):
        return remote(sums.at[st, 1 - core, j], paired.at[st, j], pair_sems, (st, j), other)

    def z_copy(st, j):
        return remote(
            zsend.at[st, j], zgot.at[st, j], z_sems, (st, j),
            shifted(at, "z", 1 if st else -1),
        )

    def y_copy(st, j):
        return remote(ysend.at[st, j], ygot.at[st, j], y_sems, (st, j), beside)

    def f_copy(st, j):
        return remote(fsend.at[st, j], fgot.at[st, j], f_sems, (st, j), other)

    def x_copy(b):
        return remote(
            xs.at[lax.rem(b, 2)],
            tiles.at[lax.div(b, 4), pl.ds(48 + lax.rem(b, 4) * 4, 4)],
            x_sems, (b,), other,
        )

    def d_copy(head):
        h, place_in = lax.rem(head, 2), lax.div(head, 2)
        return remote(
            tiles.at[h, pl.ds(16 + 2 * place_in, 2)],
            tiles.at[h, pl.ds(32 + 2 * place_in, 2)],
            d_sems, (head,), other,
        )

    def v_store(head):
        h, place_in = lax.rem(head, 2), lax.div(head, 2)
        return pltpu.make_async_copy(
            dvh_ref.at[h, 0:BLK, lanes(place_in)], gv_hbm.at[:, lanes(head)], out_sem.at[head]
        )

    def head_of(which, j):
        return which * 8 + lax.rem(j, 4) * 2 + lax.div(j, 4)

    for st in range(2):
        @pl.when(z == (0 if st else 3))
        def _(st=st):
            zgot[st] = jnp.zeros((8, HDIM, HDIM), F32)

    greet([other] + [shifted(at, axis, delta) for axis in "xyz" for delta in (1, -1)])

    def outer(lhs, rhs, head):
        return lax.dot_general(
            lhs[:, lanes(head)], rhs[:, lanes(head)], (((0,), (0,)), ((), ())),
            preferred_element_type=F32,
        )

    loads[0].wait()
    loads[1].wait()

    def theirs(j, carry):
        sums[0, 1 - core, j] = outer(qb, gb, head_of(1 - core, j))
        pair_copy(0, j).start()
        return carry

    def mine(j, carry):
        sums[0, core, j] = outer(qb, gb, head_of(core, j))
        return carry

    lax.fori_loop(0, 8, theirs, 0)
    lax.fori_loop(0, 8, mine, 0)
    loads[2].wait()
    loads[3].wait()

    def sum_keys(j):
        sums[1, 1 - core, j] = outer(kb, vb, head_of(1 - core, j))
        pair_copy(1, j).start()
        sums[1, core, j] = outer(kb, vb, head_of(core, j))

    def chain(st, j):
        pair_copy(st, j).wait_recv()

        @pl.when(z != (0 if st else 3))
        def _():
            z_copy(st, j).wait_recv()

        chip = sums[st, core, j] + paired[st, j]
        far = zgot[st, j]
        zsend[st, j] = chip + far
        full = y_lo == (0 if st else 1)
        ysend[st, j] = far + jnp.where(full, chip, 0.0)

        @pl.when(z != (3 if st else 0))
        def _():
            z_copy(st, j).start()

        y_copy(st, j).start()

    def settle(st, j):
        y_copy(st, j).wait_recv()
        both = zgot[st, j] + ygot[st, j]
        inner = 1 if st else 0
        fsend[st, j] = both + jnp.where(core != inner, sums[st, core, j], 0.0)
        f_copy(st, j).start()
        state[st, head_of(core, j)] = (
            both + jnp.where(core == inner, paired[st, j], 0.0)
        ).astype(BF16)

    def receive(st, j):
        f_copy(st, j).wait_recv()
        state[st, head_of(1 - core, j)] = fgot[st, j].astype(BF16)

    def local(head):
        q, k, g = qb[:, lanes(head)], kb[:, lanes(head)], gb[:, lanes(head)]
        q0, q1, k0, k1 = q[:HALF], q[HALF:], k[:HALF], k[HALF:]
        g0, g1 = g[:HALF], g[HALF:]
        h, first = lax.rem(head, 2), lax.div(head, 2) * 2
        tiles[h, first] = nn(upper(nt(k0, q0)), g0) + nn(nt(k0, q1).astype(BF16), g1)
        tiles[h, first + 1] = nn(upper(nt(k1, q1)), g1)

    def finish_v(head):
        h, place_in = lax.rem(head, 2), lax.div(head, 2)
        after = state[0, head]
        for part in range(2):
            rows = slice(part * HALF, part * HALF + HALF)
            index = 2 * place_in + part
            total = tiles[h, index] + nn(kb[rows, lanes(head)], after)
            rounded = total.astype(BF16)
            tiles[h, 16 + index] = rounded.astype(F32)
            dvh_ref[h, rows, lanes(place_in)] = rounded
        d_copy(head).start()
        v_store(head).start()

    def send_x(b):
        slot = lax.rem(b, 2)
        load_x(b).wait()

        @pl.when(b >= 2)
        def _():
            x_copy(b - 2).wait_send()

        theirs = pl.multiple_of((1 - core) * 256, 256)
        mine = pl.multiple_of(core * 256, 256)
        for part in range(2):
            wide = xb[slot, part * 256 : part * 256 + 256, pl.ds(theirs, 256)].astype(F32)
            for side in range(2):
                xs[slot, 2 * part + side] = wide[:, side * 128 : side * 128 + 128]
        x_copy(b).start()
        rows = pl.multiple_of(b * 256, 256)
        xt_ref[pl.ds(rows, 256), 0:BLK] = xb[slot, :, pl.ds(mine, 256)].T

        @pl.when(b < 6)
        def _():
            load_x(b + 2).start()

    def take_x(b):
        x_copy(b).wait_recv()
        rows = pl.multiple_of(b * 256, 256)
        first = 48 + lax.rem(b, 4) * 4
        for part in range(2):
            for side in range(2):
                block = tiles[lax.div(b, 4), first + 2 * part + side].astype(BF16)
                xt_ref[
                    pl.ds(rows + side * 128, 128),
                    BLK + part * 256 : BLK + part * 256 + 256,
                ] = block.T

    LAG = 3
    BEHIND = 1

    def slot_step(i, carry):
        def step(st, delay, body):
            j = i - LAG * (z if st else 3 - z) - (BEHIND if st else 0) - delay

            @pl.when(jnp.logical_and(j >= 0, j < 8))
            def _():
                body(j)

        def settled(j):
            settle(0, j)
            finish_v(head_of(core, j))

        def received(j):
            receive(0, j)
            finish_v(head_of(1 - core, j))

        step(0, 0, lambda j: chain(0, j))
        step(0, LAG, settled)
        step(0, LAG + 1, received)

        @pl.when(i < 8)
        def _():
            sum_keys(i)

        step(1, 0, lambda j: chain(1, j))
        step(1, LAG, lambda j: settle(1, j))

        @pl.when(i < 8)
        def _():
            send_x(i)
            local(head_of(core, i))
            local(head_of(1 - core, i))

        @pl.when(jnp.logical_and(i >= 8, i < 16))
        def _():
            take_x(i - 8)

        return carry

    send_sem, recv_sem = landing_refs[3 * len(UNITS) :]
    landing = {unit: landing_refs[3 * i : 3 * i + 3] for i, unit in enumerate(UNITS)}

    def piece(unit, stage, chunk):
        h, c, f = unit
        count = 4 ** (2 - stage)
        base = chunk * count
        for earlier in range(stage):
            base = base + at[ORDER[c][earlier]] * 4 ** (2 - earlier)
        start = row_start(*unit)
        return tiles.at[h, pl.ds(base, count), start : start + ROWS[(h, c)][f]]

    def hop(unit, stage, kind):
        index = UNITS.index(unit)
        axis = ORDER[unit[1]][stage]
        sign = 1 if unit[2] else -1
        mine = at[axis]
        chunk, toward = (
            (lax.rem(mine + 2, 4), sign),
            (lax.rem(mine - sign + 4, 4), -sign),
            (lax.rem(mine + sign + 4, 4), sign),
        )[kind]
        return pltpu.make_async_remote_copy(
            src_ref=piece(unit, stage, chunk),
            dst_ref=landing[unit][stage].at[kind],
            send_sem=send_sem.at[index, stage, kind],
            recv_sem=recv_sem.at[index, stage, kind],
            device_id=shifted(at, axis, toward),
            device_id_type=MESH,
        )

    def compute(h):
        def block(b, carry):
            rows = pl.multiple_of(b * 256, 256)
            z_to, y_to = lax.div(b, 2), lax.rem(b, 2)
            lhs = xt_ref[pl.ds(rows, 256), :]
            for pair in range(4):
                acc = jnp.dot(
                    lhs,
                    dvh_ref[h, :, pair * 256 : pair * 256 + 256],
                    preferred_element_type=F32,
                )
                for side in range(2):
                    tile = 2 * pair + side
                    dest = {"x": tile % 4, "y": (tile // 4) * 2 + y_to, "z": z_to}
                    for c in range(3):
                        i, j, k = (dest[axis] for axis in ORDER[c])
                        start = row_start(h, c, 0)
                        stop = start + sum(ROWS[(h, c)])
                        tiles[h, i * 16 + j * 4 + k, start:stop] = acc[
                            start:stop, side * 128 : side * 128 + 128
                        ]
            return carry

        lax.fori_loop(0, 8, block, 0)

    def units_of(h):
        return [unit for unit in UNITS if unit[0] == h]

    def issue(h, stage):
        for kind in range(2):
            for unit in units_of(h):
                hop(unit, stage, kind).start()

    def combine(h, stage):
        for unit in units_of(h):
            axis = ORDER[unit[1]][stage]
            sign = 1 if unit[2] else -1
            hop(unit, stage, 0).wait_recv()
            target = piece(unit, stage, lax.rem(at[axis] + sign + 4, 4))
            arrived = landing[unit][stage].at[0]
            if stage == 0:
                def add(i, carry, target=target, arrived=arrived):
                    four = pl.ds(i * 4, 4)
                    target[four] = target[four] + arrived[four]
                    return carry

                lax.fori_loop(0, 4, add, 0)
            else:
                target[...] = target[...] + arrived[...]
            hop(unit, stage, 2).start()

    def final(h, stage, then):
        for unit in units_of(h):
            axis = ORDER[unit[1]][stage]
            hop(unit, stage, 1).wait_recv()
            hop(unit, stage, 2).wait_recv()
            target = piece(unit, stage, at[axis])
            direct = landing[unit][stage].at[1]
            summed = landing[unit][stage].at[2]
            if stage == 0:
                def add(i, carry, target=target, direct=direct, summed=summed):
                    four = pl.ds(i * 4, 4)
                    target[four] = target[four] + direct[four] + summed[four]
                    return carry

                lax.fori_loop(0, 4, add, 0)
            elif stage == 1:
                target[...] = target[...] + direct[...] + summed[...]
            else:
                start = row_start(*unit)
                total = target[0] + direct[0] + summed[0]
                out_ref[start : start + ROWS[unit[:2]][unit[2]], h * 128 : h * 128 + 128] = (
                    total * SCALE
                )
            if then:
                hop(unit, stage + 1, 0).start()
                hop(unit, stage + 1, 1).start()

    def attend(head):
        q, k = qb[:, lanes(head)], kb[:, lanes(head)]
        v, g = vb[:, lanes(head)], gb[:, lanes(head)]
        q0, q1, k0, k1 = q[:HALF], q[HALF:], k[:HALF], k[HALF:]
        v0, v1, g0, g1 = v[:HALF], v[HALF:], g[:HALF], g[HALF:]
        after, before = state[0, head], state[1, head]
        gk0 = nn(upper(nt(v0, g0)), q0) + nn(nt(v0, g1).astype(BF16), q1) + nt(v0, after)
        gk1 = nn(upper(nt(v1, g1)), q1) + nt(v1, after)
        gq0 = nn(lower(nt(g0, v0)), k0) + nt(g0, before)
        gq1 = (
            nn(nt(g1, v0).astype(BF16), k0) + nn(lower(nt(g1, v1)), k1) + nt(g1, before)
        )
        vb[0:HALF, lanes(head)] = gk0.astype(BF16)
        vb[HALF:BLK, lanes(head)] = gk1.astype(BF16)
        gb[0:HALF, lanes(head)] = gq0.astype(BF16)
        gb[HALF:BLK, lanes(head)] = gq1.astype(BF16)

    def fill(first, last):
        def run(head, carry):
            attend(head)
            return carry

        lax.fori_loop(first, last, run, 0)

    def each(count, body):
        def run(i, carry):
            body(i)
            return carry

        lax.fori_loop(0, count, run, 0)

    def take_d(head):
        d_copy(head).wait_recv()
        h, place_in = lax.rem(head, 2), lax.div(head, 2)
        for part in range(2):
            rows = slice(BLK + part * HALF, BLK + part * HALF + HALF)
            dvh_ref[h, rows, lanes(place_in)] = tiles[h, 32 + 2 * place_in + part].astype(BF16)
        d_copy(head).wait_send()

    SPLIT = 6 + 4 * LAG

    lax.fori_loop(0, SPLIT, slot_step, 0)
    each(2, lambda b: x_copy(b + 6).wait_send())
    each(8, lambda p: take_d(2 * p))
    compute(0)
    issue(0, 0)
    lax.fori_loop(SPLIT, 8 + 4 * LAG + BEHIND, slot_step, 0)
    each(8, lambda p: take_d(2 * p + 1))
    compute(1)
    combine(0, 0)
    issue(1, 0)
    each(8, lambda j: receive(1, j))
    fill(0, 6)
    final(0, 0, True)
    fill(6, 10)
    combine(1, 0)
    fill(10, 13)
    combine(0, 1)
    fill(13, 16)
    stores = [
        pltpu.make_async_copy(gb, gq_hbm, store_sem.at[0]),
        pltpu.make_async_copy(vb, gk_hbm, store_sem.at[1]),
    ]
    for store in stores:
        store.start()
    final(0, 1, True)
    final(1, 0, True)
    combine(0, 2)
    final(0, 2, False)
    combine(1, 1)
    final(1, 1, True)
    combine(1, 2)
    final(1, 2, False)
    for unit in UNITS:
        for stage in range(3):
            for kind in range(3):
                hop(unit, stage, kind).wait_send()
    for store in stores:
        store.wait()
    each(H, lambda head: v_store(head).wait())
    for st in range(2):
        def drain(j, st=st):
            pair_copy(st, j).wait_send()
            y_copy(st, j).wait_send()
            f_copy(st, j).wait_send()

            @pl.when(z != (3 if st else 0))
            def _():
                z_copy(st, j).wait_send()

        each(8, drain)


SCALE = 65536.0 ** -0.5


def per_device(layer_input, queries, key_vectors, value_vectors, grad_output):
    arrays = (layer_input, queries, key_vectors, value_vectors, grad_output)
    wide = jax.ShapeDtypeStruct((BLK, HD), BF16)
    dma = pltpu.SemaphoreType.DMA
    hop = pltpu.VMEM((2, 8, HDIM, HDIM), F32)
    any_spec = pl.BlockSpec(memory_space=pl.ANY)
    landing = []
    for h, c, f in UNITS:
        for count in (16, 4, 1):
            landing.append(pltpu.VMEM((3, count, ROWS[(h, c)][f], 128), F32))
    gq, gk, gv, grad_weight = pl.pallas_call(
        kernel,
        out_shape=(wide, wide, wide, jax.ShapeDtypeStruct((256, 256), F32)),
        in_specs=[any_spec] * 5,
        out_specs=(any_spec,) * 3 + (pl.BlockSpec(memory_space=pltpu.VMEM),),
        scratch_shapes=[
            *[pltpu.VMEM((BLK, HD), BF16)] * 4,
            pltpu.VMEM((2048, 1024), BF16),
            pltpu.VMEM((2, 1024, 1024), BF16),
            pltpu.VMEM((2, H, HDIM, HDIM), BF16),
            pltpu.VMEM((2, 2, 8, HDIM, HDIM), F32),
            *[hop] * 7,
            pltpu.VMEM((2, BLK, 512), BF16),
            pltpu.VMEM((2, 4, 256, 128), F32),
            pltpu.VMEM((2, 64, 256, 128), F32),
            dma((4,)), dma((2,)), dma((H,)), dma((2,)),
            *[dma((2, 8))] * 8,
            dma((8,)), dma((8,)), dma((H,)), dma((H,)),
            *landing,
            dma((len(UNITS), 3, 3)), dma((len(UNITS), 3, 3)),
        ],
        compiler_params=pltpu.CompilerParams(
            collective_id=1, has_side_effects=True, vmem_limit_bytes=63 << 20
        ),
        name="fused",
    )(*(array[0] for array in arrays))
    return (gq[None], gk[None], gv[None], grad_weight)


def solution(mesh):
    return jax.shard_map(
        per_device,
        mesh=mesh,
        in_specs=(
            P("grp", "seq", None),
            P("grp", "seq", None),
            P("grp", "seq", None),
            P("grp", "seq", None),
            P("grp", "seq", None),
        ),
        out_specs=(
            P("grp", "seq", None),
            P("grp", "seq", None),
            P("grp", "seq", None),
            P("seq", "grp"),
        ),
        check_vma=False,
    )
```

```python
import jax
import jax.numpy as jnp
from jax import lax
from jax.experimental import pallas as pl
from jax.experimental.pallas import tpu as pltpu
from jax.sharding import PartitionSpec as P

MESH = pl.DeviceIdType.MESH
H = 16
HDIM = 128
BLK = 512
HD = 2048
F32 = jnp.float32
BF16 = jnp.bfloat16

ROWS = {
    (0, 0): (48, 40), (0, 1): (40, 48), (0, 2): (40, 40),
    (1, 0): (40, 48), (1, 1): (48, 40), (1, 2): (40, 40),
}
ORDER = (("x", "y", "z"), ("y", "z", "x"), ("z", "x", "y"))
UNITS = [(h, c, f) for h in range(2) for c in range(3) for f in range(2)]


def row_start(h, c, f):
    start = sum(sum(ROWS[(h, prior)]) for prior in range(c))
    return start + (ROWS[(h, c)][0] if f else 0)


def place():
    seq, grp = lax.axis_index("seq"), lax.axis_index("grp")
    core = lax.rem(seq, 2)
    y_lo = lax.rem(lax.div(seq, 2), 2)
    return {
        "x": lax.rem(grp, 4),
        "y": lax.div(grp, 4) * 2 + y_lo,
        "z": lax.div(seq, 4),
        "core": core,
    }


def device(at):
    return (
        at["z"] * 4 + lax.rem(at["y"], 2) * 2 + at["core"],
        lax.div(at["y"], 2) * 4 + at["x"],
    )


def shifted(at, axis, delta):
    moved = dict(at)
    moved[axis] = lax.rem(at[axis] + delta + 4, 4)
    return device(moved)


def partner_of(at):
    moved = dict(at)
    moved["core"] = 1 - at["core"]
    return device(moved)


def greet(devices):
    barrier = pltpu.get_barrier_semaphore()
    for other in devices:
        pl.semaphore_signal(barrier, inc=1, device_id=other, device_id_type=MESH)
    pl.semaphore_wait(barrier, len(devices))


def lanes(head):
    return pl.ds(pl.multiple_of(head * HDIM, HDIM), HDIM)


def nt(lhs, rhs):
    return lax.dot_general(lhs, rhs, (((1,), (1,)), ((), ())), preferred_element_type=F32)


def nn(lhs, rhs):
    return jnp.dot(lhs, rhs, preferred_element_type=F32)


HALF = BLK // 2


def lower(block):
    row = lax.broadcasted_iota(jnp.int32, (HALF, HALF), 0)
    col = lax.broadcasted_iota(jnp.int32, (HALF, HALF), 1)
    return jnp.where(col <= row, block, 0.0).astype(BF16)


def upper(block):
    row = lax.broadcasted_iota(jnp.int32, (HALF, HALF), 0)
    col = lax.broadcasted_iota(jnp.int32, (HALF, HALF), 1)
    return jnp.where(row <= col, block, 0.0).astype(BF16)


def kernel(
    x_hbm, q_hbm, k_hbm, v_hbm, g_hbm,
    gq_hbm, gk_hbm, gv_hbm, out_ref,
    qb, kb, vb, gb, xt_ref, dvh_ref, state,
    sums, paired, zgot, zsend, ygot, ysend, fgot, fsend, xb, xs, tiles,
    load_sem, xload_sem, out_sem, store_sem,
    pair_send, pair_recv, z_send, z_recv, y_send, y_recv, f_send, f_recv,
    x_send, x_recv, d_send, d_recv, *landing_refs
):
    pair_sems, z_sems, y_sems = (pair_send, pair_recv), (z_send, z_recv), (y_send, y_recv)
    f_sems, x_sems, d_sems = (f_send, f_recv), (x_send, x_recv), (d_send, d_recv)
    at = place()
    core = at["core"]
    z = at["z"]
    y_lo = lax.rem(at["y"], 2)
    other = partner_of(at)
    beside = dict(at)
    beside["y"] = at["y"] + 1 - 2 * y_lo
    beside = device(beside)

    loads = [
        pltpu.make_async_copy(src, dst, load_sem.at[i])
        for i, (src, dst) in enumerate(
            ((q_hbm, qb), (g_hbm, gb), (k_hbm, kb), (v_hbm, vb))
        )
    ]
    for load in loads:
        load.start()

    def load_x(b):
        cols = pl.multiple_of(b * 512, 512)
        slot = lax.rem(b, 2)
        return pltpu.make_async_copy(
            x_hbm.at[:, pl.ds(cols, 512)], xb.at[slot], xload_sem.at[slot]
        )

    load_x(0).start()
    load_x(1).start()

    def remote(src, dst, sems, index, target):
        send, recv = sems
        for i in index:
            send, recv = send.at[i], recv.at[i]
        return pltpu.make_async_remote_copy(
            src_ref=src, dst_ref=dst, send_sem=send, recv_sem=recv,
            device_id=target, device_id_type=MESH,
        )

    def pair_copy(st, j):
        return remote(sums.at[st, 1 - core, j], paired.at[st, j], pair_sems, (st, j), other)

    def z_copy(st, j):
        return remote(
            zsend.at[st, j], zgot.at[st, j], z_sems, (st, j),
            shifted(at, "z", 1 if st else -1),
        )

    def y_copy(st, j):
        return remote(ysend.at[st, j], ygot.at[st, j], y_sems, (st, j), beside)

    def f_copy(st, j):
        return remote(fsend.at[st, j], fgot.at[st, j], f_sems, (st, j), other)

    def x_copy(b):
        return remote(
            xs.at[lax.rem(b, 2)],
            tiles.at[lax.div(b, 4), pl.ds(48 + lax.rem(b, 4) * 4, 4)],
            x_sems, (b,), other,
        )

    def d_copy(head):
        h, place_in = lax.rem(head, 2), lax.div(head, 2)
        return remote(
            tiles.at[h, pl.ds(16 + 2 * place_in, 2)],
            tiles.at[h, pl.ds(32 + 2 * place_in, 2)],
            d_sems, (head,), other,
        )

    def v_store(head):
        h, place_in = lax.rem(head, 2), lax.div(head, 2)
        return pltpu.make_async_copy(
            dvh_ref.at[h, 0:BLK, lanes(place_in)], gv_hbm.at[:, lanes(head)], out_sem.at[head]
        )

    def head_of(which, j):
        return which * 8 + lax.rem(j, 4) * 2 + lax.div(j, 4)

    for st in range(2):
        @pl.when(z == (0 if st else 3))
        def _(st=st):
            zgot[st] = jnp.zeros((8, HDIM, HDIM), F32)

    greet([other] + [shifted(at, axis, delta) for axis in "xyz" for delta in (1, -1)])

    def outer(lhs, rhs, head):
        return lax.dot_general(
            lhs[:, lanes(head)], rhs[:, lanes(head)], (((0,), (0,)), ((), ())),
            preferred_element_type=F32,
        )

    loads[0].wait()
    loads[1].wait()

    def theirs(j, carry):
        sums[0, 1 - core, j] = outer(qb, gb, head_of(1 - core, j))
        pair_copy(0, j).start()
        return carry

    def mine(j, carry):
        sums[0, core, j] = outer(qb, gb, head_of(core, j))
        return carry

    lax.fori_loop(0, 8, theirs, 0)
    lax.fori_loop(0, 8, mine, 0)
    loads[2].wait()
    loads[3].wait()

    def sum_keys(j):
        sums[1, 1 - core, j] = outer(kb, vb, head_of(1 - core, j))
        pair_copy(1, j).start()
        sums[1, core, j] = outer(kb, vb, head_of(core, j))

    def chain(st, j):
        pair_copy(st, j).wait_recv()

        @pl.when(z != (0 if st else 3))
        def _():
            z_copy(st, j).wait_recv()

        chip = sums[st, core, j] + paired[st, j]
        far = zgot[st, j]
        zsend[st, j] = chip + far
        full = y_lo == (0 if st else 1)
        ysend[st, j] = far + jnp.where(full, chip, 0.0)

        @pl.when(z != (3 if st else 0))
        def _():
            z_copy(st, j).start()

        y_copy(st, j).start()

    def settle(st, j):
        y_copy(st, j).wait_recv()
        both = zgot[st, j] + ygot[st, j]
        inner = 1 if st else 0
        fsend[st, j] = both + jnp.where(core != inner, sums[st, core, j], 0.0)
        f_copy(st, j).start()
        state[st, head_of(core, j)] = (
            both + jnp.where(core == inner, paired[st, j], 0.0)
        ).astype(BF16)

    def receive(st, j):
        f_copy(st, j).wait_recv()
        state[st, head_of(1 - core, j)] = fgot[st, j].astype(BF16)

    def local(head):
        q, k, g = qb[:, lanes(head)], kb[:, lanes(head)], gb[:, lanes(head)]
        q0, q1, k0, k1 = q[:HALF], q[HALF:], k[:HALF], k[HALF:]
        g0, g1 = g[:HALF], g[HALF:]
        h, first = lax.rem(head, 2), lax.div(head, 2) * 2
        tiles[h, first] = nn(upper(nt(k0, q0)), g0) + nn(nt(k0, q1).astype(BF16), g1)
        tiles[h, first + 1] = nn(upper(nt(k1, q1)), g1)

    def finish_v(head):
        h, place_in = lax.rem(head, 2), lax.div(head, 2)
        after = state[0, head]
        for part in range(2):
            rows = slice(part * HALF, part * HALF + HALF)
            index = 2 * place_in + part
            total = tiles[h, index] + nn(kb[rows, lanes(head)], after)
            rounded = total.astype(BF16)
            tiles[h, 16 + index] = rounded.astype(F32)
            dvh_ref[h, rows, lanes(place_in)] = rounded
        d_copy(head).start()
        v_store(head).start()

    def send_x(b):
        slot = lax.rem(b, 2)
        load_x(b).wait()

        @pl.when(b >= 2)
        def _():
            x_copy(b - 2).wait_send()

        theirs = pl.multiple_of((1 - core) * 256, 256)
        mine = pl.multiple_of(core * 256, 256)
        for part in range(2):
            wide = xb[slot, part * 256 : part * 256 + 256, pl.ds(theirs, 256)].astype(F32)
            for side in range(2):
                xs[slot, 2 * part + side] = wide[:, side * 128 : side * 128 + 128]
        x_copy(b).start()
        rows = pl.multiple_of(b * 256, 256)
        xt_ref[pl.ds(rows, 256), 0:BLK] = xb[slot, :, pl.ds(mine, 256)].T

        @pl.when(b < 6)
        def _():
            load_x(b + 2).start()

    def take_x(b):
        x_copy(b).wait_recv()
        rows = pl.multiple_of(b * 256, 256)
        first = 48 + lax.rem(b, 4) * 4
        for part in range(2):
            for side in range(2):
                block = tiles[lax.div(b, 4), first + 2 * part + side].astype(BF16)
                xt_ref[
                    pl.ds(rows + side * 128, 128),
                    BLK + part * 256 : BLK + part * 256 + 256,
                ] = block.T

    LAG = 3
    BEHIND = 1

    def slot_step(i, carry):
        def step(st, delay, body):
            j = i - LAG * (z if st else 3 - z) - (BEHIND if st else 0) - delay

            @pl.when(jnp.logical_and(j >= 0, j < 8))
            def _():
                body(j)

        def settled(j):
            settle(0, j)
            finish_v(head_of(core, j))

        def received(j):
            receive(0, j)
            finish_v(head_of(1 - core, j))

        step(0, 0, lambda j: chain(0, j))
        step(0, LAG, settled)
        step(0, LAG + 1, received)

        @pl.when(i < 8)
        def _():
            sum_keys(i)

        step(1, 0, lambda j: chain(1, j))
        step(1, LAG, lambda j: settle(1, j))

        @pl.when(i < 8)
        def _():
            send_x(i)
            local(head_of(core, i))
            local(head_of(1 - core, i))

        @pl.when(jnp.logical_and(i >= 8, i < 16))
        def _():
            take_x(i - 8)

        return carry

    send_sem, recv_sem = landing_refs[3 * len(UNITS) :]
    landing = {unit: landing_refs[3 * i : 3 * i + 3] for i, unit in enumerate(UNITS)}

    def piece(unit, stage, chunk):
        h, c, f = unit
        count = 4 ** (2 - stage)
        base = chunk * count
        for earlier in range(stage):
            base = base + at[ORDER[c][earlier]] * 4 ** (2 - earlier)
        start = row_start(*unit)
        return tiles.at[h, pl.ds(base, count), start : start + ROWS[(h, c)][f]]

    def hop(unit, stage, kind):
        index = UNITS.index(unit)
        axis = ORDER[unit[1]][stage]
        sign = 1 if unit[2] else -1
        mine = at[axis]
        chunk, toward = (
            (lax.rem(mine + 2, 4), sign),
            (lax.rem(mine - sign + 4, 4), -sign),
            (lax.rem(mine + sign + 4, 4), sign),
        )[kind]
        return pltpu.make_async_remote_copy(
            src_ref=piece(unit, stage, chunk),
            dst_ref=landing[unit][stage].at[kind],
            send_sem=send_sem.at[index, stage, kind],
            recv_sem=recv_sem.at[index, stage, kind],
            device_id=shifted(at, axis, toward),
            device_id_type=MESH,
        )

    def compute(h):
        def block(b, carry):
            rows = pl.multiple_of(b * 256, 256)
            z_to, y_to = lax.div(b, 2), lax.rem(b, 2)
            lhs = xt_ref[pl.ds(rows, 256), :]
            for pair in range(4):
                acc = jnp.dot(
                    lhs,
                    dvh_ref[h, :, pair * 256 : pair * 256 + 256],
                    preferred_element_type=F32,
                )
                for side in range(2):
                    tile = 2 * pair + side
                    dest = {"x": tile % 4, "y": (tile // 4) * 2 + y_to, "z": z_to}
                    for c in range(3):
                        i, j, k = (dest[axis] for axis in ORDER[c])
                        start = row_start(h, c, 0)
                        stop = start + sum(ROWS[(h, c)])
                        tiles[h, i * 16 + j * 4 + k, start:stop] = acc[
                            start:stop, side * 128 : side * 128 + 128
                        ]
            return carry

        lax.fori_loop(0, 8, block, 0)

    def units_of(h):
        return [unit for unit in UNITS if unit[0] == h]

    def issue(h, stage):
        for kind in range(2):
            for unit in units_of(h):
                hop(unit, stage, kind).start()

    def combine(h, stage):
        for unit in units_of(h):
            axis = ORDER[unit[1]][stage]
            sign = 1 if unit[2] else -1
            hop(unit, stage, 0).wait_recv()
            target = piece(unit, stage, lax.rem(at[axis] + sign + 4, 4))
            arrived = landing[unit][stage].at[0]
            if stage == 0:
                def add(i, carry, target=target, arrived=arrived):
                    four = pl.ds(i * 4, 4)
                    target[four] = target[four] + arrived[four]
                    return carry

                lax.fori_loop(0, 4, add, 0)
            else:
                target[...] = target[...] + arrived[...]
            hop(unit, stage, 2).start()

    def final(h, stage, then):
        for unit in units_of(h):
            axis = ORDER[unit[1]][stage]
            hop(unit, stage, 1).wait_recv()
            hop(unit, stage, 2).wait_recv()
            target = piece(unit, stage, at[axis])
            direct = landing[unit][stage].at[1]
            summed = landing[unit][stage].at[2]
            if stage == 0:
                def add(i, carry, target=target, direct=direct, summed=summed):
                    four = pl.ds(i * 4, 4)
                    target[four] = target[four] + direct[four] + summed[four]
                    return carry

                lax.fori_loop(0, 4, add, 0)
            elif stage == 1:
                target[...] = target[...] + direct[...] + summed[...]
            else:
                start = row_start(*unit)
                total = target[0] + direct[0] + summed[0]
                out_ref[start : start + ROWS[unit[:2]][unit[2]], h * 128 : h * 128 + 128] = (
                    total * SCALE
                )
            if then:
                hop(unit, stage + 1, 0).start()
                hop(unit, stage + 1, 1).start()

    def attend(head):
        q, k = qb[:, lanes(head)], kb[:, lanes(head)]
        v, g = vb[:, lanes(head)], gb[:, lanes(head)]
        q0, q1, k0, k1 = q[:HALF], q[HALF:], k[:HALF], k[HALF:]
        v0, v1, g0, g1 = v[:HALF], v[HALF:], g[:HALF], g[HALF:]
        after, before = state[0, head], state[1, head]
        gk0 = nn(upper(nt(v0, g0)), q0) + nn(nt(v0, g1).astype(BF16), q1) + nt(v0, after)
        gk1 = nn(upper(nt(v1, g1)), q1) + nt(v1, after)
        gq0 = nn(lower(nt(g0, v0)), k0) + nt(g0, before)
        gq1 = (
            nn(nt(g1, v0).astype(BF16), k0) + nn(lower(nt(g1, v1)), k1) + nt(g1, before)
        )
        vb[0:HALF, lanes(head)] = gk0.astype(BF16)
        vb[HALF:BLK, lanes(head)] = gk1.astype(BF16)
        gb[0:HALF, lanes(head)] = gq0.astype(BF16)
        gb[HALF:BLK, lanes(head)] = gq1.astype(BF16)

    def fill(first, last):
        def run(head, carry):
            attend(head)
            return carry

        lax.fori_loop(first, last, run, 0)

    def each(count, body):
        def run(i, carry):
            body(i)
            return carry

        lax.fori_loop(0, count, run, 0)

    def take_d(head):
        d_copy(head).wait_recv()
        h, place_in = lax.rem(head, 2), lax.div(head, 2)
        for part in range(2):
            rows = slice(BLK + part * HALF, BLK + part * HALF + HALF)
            dvh_ref[h, rows, lanes(place_in)] = tiles[h, 32 + 2 * place_in + part].astype(BF16)
        d_copy(head).wait_send()

    SPLIT = 6 + 4 * LAG

    lax.fori_loop(0, SPLIT, slot_step, 0)
    each(2, lambda b: x_copy(b + 6).wait_send())
    each(8, lambda p: take_d(2 * p))
    compute(0)
    issue(0, 0)
    lax.fori_loop(SPLIT, 8 + 4 * LAG + BEHIND, slot_step, 0)
    each(8, lambda p: take_d(2 * p + 1))
    compute(1)
    combine(0, 0)
    issue(1, 0)
    each(8, lambda j: receive(1, j))
    fill(0, 6)
    final(0, 0, True)
    fill(6, 10)
    combine(1, 0)
    fill(10, 13)
    combine(0, 1)
    fill(13, 16)
    stores = [
        pltpu.make_async_copy(gb, gq_hbm, store_sem.at[0]),
        pltpu.make_async_copy(vb, gk_hbm, store_sem.at[1]),
    ]
    for store in stores:
        store.start()
    final(1, 0, True)
    final(0, 1, True)
    combine(1, 1)
    combine(0, 2)
    final(1, 1, True)
    final(0, 2, False)
    combine(1, 2)
    final(1, 2, False)
    for unit in UNITS:
        for stage in range(3):
            for kind in range(3):
                hop(unit, stage, kind).wait_send()
    for store in stores:
        store.wait()
    each(H, lambda head: v_store(head).wait())
    for st in range(2):
        def drain(j, st=st):
            pair_copy(st, j).wait_send()
            y_copy(st, j).wait_send()
            f_copy(st, j).wait_send()

            @pl.when(z != (3 if st else 0))
            def _():
                z_copy(st, j).wait_send()

        each(8, drain)


SCALE = 65536.0 ** -0.5


def per_device(layer_input, queries, key_vectors, value_vectors, grad_output):
    arrays = (layer_input, queries, key_vectors, value_vectors, grad_output)
    wide = jax.ShapeDtypeStruct((BLK, HD), BF16)
    dma = pltpu.SemaphoreType.DMA
    hop = pltpu.VMEM((2, 8, HDIM, HDIM), F32)
    any_spec = pl.BlockSpec(memory_space=pl.ANY)
    landing = []
    for h, c, f in UNITS:
        for count in (16, 4, 1):
            landing.append(pltpu.VMEM((3, count, ROWS[(h, c)][f], 128), F32))
    gq, gk, gv, grad_weight = pl.pallas_call(
        kernel,
        out_shape=(wide, wide, wide, jax.ShapeDtypeStruct((256, 256), F32)),
        in_specs=[any_spec] * 5,
        out_specs=(any_spec,) * 3 + (pl.BlockSpec(memory_space=pltpu.VMEM),),
        scratch_shapes=[
            *[pltpu.VMEM((BLK, HD), BF16)] * 4,
            pltpu.VMEM((2048, 1024), BF16),
            pltpu.VMEM((2, 1024, 1024), BF16),
            pltpu.VMEM((2, H, HDIM, HDIM), BF16),
            pltpu.VMEM((2, 2, 8, HDIM, HDIM), F32),
            *[hop] * 7,
            pltpu.VMEM((2, BLK, 512), BF16),
            pltpu.VMEM((2, 4, 256, 128), F32),
            pltpu.VMEM((2, 64, 256, 128), F32),
            dma((4,)), dma((2,)), dma((H,)), dma((2,)),
            *[dma((2, 8))] * 8,
            dma((8,)), dma((8,)), dma((H,)), dma((H,)),
            *landing,
            dma((len(UNITS), 3, 3)), dma((len(UNITS), 3, 3)),
        ],
        compiler_params=pltpu.CompilerParams(
            collective_id=1, has_side_effects=True, vmem_limit_bytes=63 << 20
        ),
        name="fused",
    )(*(array[0] for array in arrays))
    return (gq[None], gk[None], gv[None], grad_weight)


def solution(mesh):
    return jax.shard_map(
        per_device,
        mesh=mesh,
        in_specs=(
            P("grp", "seq", None),
            P("grp", "seq", None),
            P("grp", "seq", None),
            P("grp", "seq", None),
            P("grp", "seq", None),
        ),
        out_specs=(
            P("grp", "seq", None),
            P("grp", "seq", None),
            P("grp", "seq", None),
            P("seq", "grp"),
        ),
        check_vma=False,
    )
```
